128 devices in a mesh: seq: 16 (over z, y_lo, core), head: 8 (over x, y_hi).
Axes of the slice: x: 4, y: 4 (y_hi: 2, y_lo: 2; y = y_hi * 2 + y_lo), z: 4, core: 2. Of those that a mesh axis runs over, the one named last changes fastest.
Arguments:
- queries: bfloat16 [32768, 4096], P(('seq', 'head')), may hold values from -6 to 6
- key_rows: bfloat16 [32768, 2048], P(('seq', 'head')), may hold values from -6 to 6
- value_rows: bfloat16 [32768, 2048], P(('seq', 'head')), may hold values from -6 to 6
- output_grad: bfloat16 [32768, 4096], P(('seq', 'head')), may hold values from -6 to 6
Outputs:
- query_grad: bfloat16 [32768, 4096], P(('seq', 'head'))
- key_grad: bfloat16 [32768, 2048], P(('seq', 'head'))
- value_grad: bfloat16 [32768, 2048], P(('seq', 'head'))
The draws below stay inside these ranges and needn't reach their ends.
All inputs are finite; a program needn't handle non-finite values.
Results may differ from the reference program's by a relative error of at most 0.012.
Values may be sent and summed in bfloat16 or wider, within the bound.
A program may use at most 256 MiB of HBM per device.

```python
import math
import jax
import jax.numpy as jnp
from jax import lax

Q_HEADS = 32
KV_HEADS = 16
HEAD_DIM = 128
WINDOW = 1024
GROUP = 2
TOKENS = 32768


def draw_queries(key, part):
    shape_three = (TOKENS, Q_HEADS, HEAD_DIM)
    drawn_values = jnp.clip(jax.random.normal(jax.random.fold_in(key, 11), shape_three, jnp.float32), -6.0, 6.0)
    return drawn_values.reshape(TOKENS, Q_HEADS * HEAD_DIM).astype(jnp.bfloat16)


def draw_key_rows(key, part):
    shape_three = (TOKENS, KV_HEADS, HEAD_DIM)
    drawn_values = jnp.clip(jax.random.normal(jax.random.fold_in(key, 13), shape_three, jnp.float32), -6.0, 6.0)
    return drawn_values.reshape(TOKENS, KV_HEADS * HEAD_DIM).astype(jnp.bfloat16)


def shard_levels(own_key, shape, cuts, least, top_value):
    def one(position, blocks):
        heights = jax.random.uniform(jax.random.fold_in(jax.random.fold_in(own_key, 6), position), (blocks,), jnp.float32, least / len(cuts), top_value / len(cuts))
        return jnp.repeat(jnp.exp(heights), shape[position] // blocks).reshape((-1,) + (1,) * (len(shape) - position - 1))

    level = one(*cuts[0])
    for cut in cuts[1:]:
        level = level * one(*cut)
    return level


def gaussian(stream_key, extent, scale, limit, shards=(), kind=jnp.bfloat16):
    entries = jax.random.normal(stream_key, extent, jnp.float32) * scale
    if len(shards) > 0:
        entries = shard_levels(stream_key, extent, shards, -0.22, 0.18) * entries
    return jnp.clip(entries, min=-limit, max=limit).astype(kind)


def setup_inputs(seed: int = 0) -> dict:
    arg_keys = jax.random.split(jax.random.key(seed), 5)
    queries = draw_queries(jax.random.fold_in(arg_keys[4], 71), 0)
    key_rows = draw_key_rows(jax.random.fold_in(arg_keys[4], 71), 0)
    value_rows = gaussian(arg_keys[2], (TOKENS, KV_HEADS * HEAD_DIM), 1.0, 6.0, ((0, 128),))
    output_grad = gaussian(arg_keys[3], (TOKENS, Q_HEADS * HEAD_DIM), 1.0, 6.0, ((0, 128),))
    return dict(queries=queries, key_rows=key_rows, value_rows=value_rows, output_grad=output_grad)


score_scale = 168.0 ** -0.5


def band_mask(query_pos, key_pos):
    offset = query_pos[:, None] - key_pos[None, :]
    return (offset >= 0) & (offset < WINDOW) & (key_pos[None, :] >= 0)


def block_grads(query_block, key_block, value_block, grad_block, allowed):
    query_wide = query_block.astype(jnp.float32)
    key_wide = key_block.astype(jnp.float32)
    value_wide = value_block.astype(jnp.float32)
    grad_wide = grad_block.astype(jnp.float32)
    scores = jnp.einsum("qhgd,khd->hgqk", query_wide, key_wide) * score_scale
    scores = jnp.where(allowed, scores, -jnp.inf)
    row_peak = jnp.max(scores, axis=-1, keepdims=True)
    raised = jnp.exp(scores - row_peak)
    probability = raised / jnp.sum(raised, axis=-1, keepdims=True)
    prob_grad = jnp.einsum("qhgd,khd->hgqk", grad_wide, value_wide)
    row_centre = jnp.sum(probability * prob_grad, axis=-1, keepdims=True)
    score_grad = (probability * (prob_grad - row_centre)).astype(jnp.bfloat16).astype(jnp.float32)
    prob_low = probability.astype(jnp.bfloat16).astype(jnp.float32)
    query_part = jnp.einsum("hgqk,khd->qhgd", score_grad, key_wide) * score_scale
    key_part = jnp.einsum("hgqk,qhgd->khd", score_grad, query_wide) * score_scale
    value_part = jnp.einsum("hgqk,qhgd->khd", prob_low, grad_wide)
    return query_part, key_part, value_part


def reference(queries, key_rows, value_rows, output_grad):
    token_count = queries.shape[0]
    query_heads = queries.reshape(token_count, KV_HEADS, GROUP, HEAD_DIM)
    grad_heads = output_grad.reshape(token_count, KV_HEADS, GROUP, HEAD_DIM)
    zero_rows = jnp.zeros((WINDOW, KV_HEADS, HEAD_DIM), key_rows.dtype)
    key_ext = jnp.concatenate([zero_rows, key_rows.reshape(token_count, KV_HEADS, HEAD_DIM)], axis=0)
    value_ext = jnp.concatenate([zero_rows, value_rows.reshape(token_count, KV_HEADS, HEAD_DIM)], axis=0)
    block_rows = math.gcd(token_count, 512)
    span = block_rows + WINDOW

    def scan_step(totals, block_index):
        key_acc, value_acc = totals
        begin_row = block_index * block_rows
        query_block = lax.dynamic_slice_in_dim(query_heads, begin_row, block_rows, 0)
        grad_block = lax.dynamic_slice_in_dim(grad_heads, begin_row, block_rows, 0)
        key_block = lax.dynamic_slice_in_dim(key_ext, begin_row, span, 0)
        value_block = lax.dynamic_slice_in_dim(value_ext, begin_row, span, 0)
        query_pos = begin_row + jnp.arange(block_rows, dtype=jnp.int32)
        key_pos = begin_row - WINDOW + jnp.arange(span, dtype=jnp.int32)
        allowed = band_mask(query_pos, key_pos)
        query_part, key_part, value_part = block_grads(query_block, key_block, value_block, grad_block, allowed)
        key_acc = lax.dynamic_update_slice_in_dim(key_acc, lax.dynamic_slice_in_dim(key_acc, begin_row, span, 0) + key_part, begin_row, 0)
        value_acc = lax.dynamic_update_slice_in_dim(value_acc, lax.dynamic_slice_in_dim(value_acc, begin_row, span, 0) + value_part, begin_row, 0)
        return (key_acc, value_acc), query_part.astype(jnp.bfloat16)

    start_totals = (jnp.zeros(key_ext.shape, jnp.float32), jnp.zeros(value_ext.shape, jnp.float32))
    block_ids = jnp.arange(token_count // block_rows, dtype=jnp.int32)
    (key_acc, value_acc), query_parts = lax.scan(scan_step, start_totals, block_ids)
    query_grad = query_parts.reshape(token_count, Q_HEADS * HEAD_DIM)
    key_grad = key_acc[WINDOW:].astype(jnp.bfloat16).reshape(token_count, KV_HEADS * HEAD_DIM)
    value_grad = value_acc[WINDOW:].astype(jnp.bfloat16).reshape(token_count, KV_HEADS * HEAD_DIM)
    return query_grad, key_grad, value_grad
```

```python
import functools
import math

import jax
import jax.numpy as jnp
from jax import lax
from jax.experimental import pallas as pl
from jax.experimental.pallas import tpu as pltpu
from jax.sharding import PartitionSpec as P

HEAD_DIM = 128
WINDOW = 1024
GROUP = 2
SCALE = 168.0 ** (-0.5)
LOG2E = math.log2(math.e)
NEG = -1e30

ROWS = 256
HALO = WINDOW // ROWS
SPAN = HALO + 1
HEADS_KV = 2
PAIR = GROUP * HEAD_DIM
MESH = pl.DeviceIdType.MESH
PEERS = ((2, 1), (1, 1), (3, 1), (2, 0), (0, 1), (1, 0), (3, 0))


def rows_of(index, count):
    return pl.ds(pl.multiple_of(index * count, count), count)


def fold(op, value):
    out = value[0:8]
    for begin in range(8, value.shape[0], 8):
        out = op(out, value[begin : begin + 8])
    return out


def kernel(
    seq_count,
    q_hbm,
    k_hbm,
    v_hbm,
    g_hbm,
    dq_hbm,
    dk_hbm,
    dv_hbm,
    qg,
    kv,
    dkv,
    dkv_low,
    halo_in,
    dq_low,
    s_buf,
    g_buf,
    p_low,
    s_low,
    qg_sem,
    kv_sem,
    in_send,
    halo_send,
    halo_recv,
    back_send,
    back_recv,
    out_send,
    out_recv,
    own_sem,
):
    s, h = lax.axis_index("seq"), lax.axis_index("head")
    x, y = h // 2, lax.rem(h, 2)
    after = (lax.rem(s + 1, seq_count), h)
    before = (lax.rem(s + seq_count - 1, seq_count), h)
    peers = []
    for dx, dy in PEERS:
        across = lax.rem(y + dy, 2)
        peers.append(lax.rem(x + dx, 4) * 2 + across)

    barrier = pltpu.get_barrier_semaphore()
    for peer in peers:
        pl.semaphore_signal(barrier, inc=1, device_id=(s, peer), device_id_type=MESH)
    for device in (after, before):
        pl.semaphore_signal(barrier, inc=1, device_id=device, device_id_type=MESH)
    pl.semaphore_wait(barrier, len(PEERS) + 2)

    def kv_parts(j, owner):
        col = pl.multiple_of((owner * HEADS_KV + j) * HEAD_DIM, HEAD_DIM)
        for part, ref in enumerate((k_hbm, v_hbm)):
            yield (
                ref.at[:, pl.ds(col, HEAD_DIM)],
                kv.at[j, HALO + h, :, part * HEAD_DIM : (part + 1) * HEAD_DIM],
            )

    def qg_parts(j, owner, piece):
        col = pl.multiple_of((owner * HEADS_KV + j) * PAIR, PAIR)
        half = slice(piece * (ROWS // 2), (piece + 1) * (ROWS // 2))
        for part, ref in enumerate((q_hbm, g_hbm)):
            yield (
                ref.at[half, pl.ds(col, PAIR)],
                qg.at[j, h, half, part * PAIR : (part + 1) * PAIR],
            )

    def push(src, dst, send, recv, device):
        pltpu.make_async_remote_copy(
            src_ref=src, dst_ref=dst, send_sem=send, recv_sem=recv, device_id=device, device_id_type=MESH
        ).start()

    def push_kv(j):
        for part in range(2):
            for n, peer in enumerate(peers):
                src, dst = list(kv_parts(j, peer))[part]
                push(src, dst, in_send.at[n], kv_sem.at[j, h], (s, peer))

    def push_qg(j):
        for piece in range(2):
            for part in range(2):
                for n, peer in enumerate(peers):
                    src, dst = list(qg_parts(j, peer, piece))[part]
                    push(src, dst, in_send.at[n], qg_sem.at[j, h], (s, peer))

    def got(ref, sem):
        pltpu.make_async_copy(ref, ref, sem).wait()

    push_kv(0)
    push_kv(1)
    push_qg(0)
    for j in range(HEADS_KV):
        for src, dst in kv_parts(j, h):
            pltpu.make_async_copy(src, dst, kv_sem.at[j, h]).start()
        for piece in range(2):
            for src, dst in qg_parts(j, h, piece):
                pltpu.make_async_copy(src, dst, qg_sem.at[j, h]).start()

    def clear(b, carry):
        for j in range(HEADS_KV):
            dkv[j, b] = jnp.zeros((ROWS, 2 * HEAD_DIM), jnp.float32)
        return carry

    lax.fori_loop(0, 3 * HALO, clear, 0)

    for j in range(HEADS_KV):
        for r in range(8):
            got(kv.at[j, HALO + r], kv_sem.at[j, r])
        for b in range(HALO):
            push(kv.at[j, 8 + b], kv.at[j, b], halo_send.at[j], halo_recv.at[j], after)
    push_qg(1)

    key_row = lax.broadcasted_iota(jnp.int32, (ROWS, ROWS), 0)
    query_col = lax.broadcasted_iota(jnp.int32, (ROWS, ROWS), 1)

    def unit(j, r):
        keys = kv[j, pl.ds(r, SPAN), :, 0:HEAD_DIM].reshape(SPAN * ROWS, HEAD_DIM)
        values = kv[j, pl.ds(r, SPAN), :, HEAD_DIM:].reshape(SPAN * ROWS, HEAD_DIM)
        for hh in range(GROUP):
            query = qg[j, r, :, hh * HEAD_DIM : (hh + 1) * HEAD_DIM]
            grad = qg[j, r, :, PAIR + hh * HEAD_DIM : PAIR + (hh + 1) * HEAD_DIM]
            nt = (((1,), (1,)), ((), ()))
            s_buf[...] = lax.dot_general(keys, query, nt, preferred_element_type=jnp.float32)
            g_buf[...] = lax.dot_general(values, grad, nt, preferred_element_type=jnp.float32)
            peak = jnp.full((8, ROWS), NEG, jnp.float32)
            for c in range(SPAN):
                part = s_buf[c * ROWS : (c + 1) * ROWS]
                if c < HALO:
                    inside = (s > 0) | (r + c >= HALO)
                    if c == 0:
                        part = jnp.where((key_row > query_col) & inside, part, NEG)
                    else:
                        part = jnp.where(inside, part, NEG)
                else:
                    part = jnp.where(key_row <= query_col, part, NEG)
                s_buf[c * ROWS : (c + 1) * ROWS] = part
                peak = jnp.maximum(peak, fold(jnp.maximum, part))
            peak = jnp.max(peak, axis=0, keepdims=True)
            total = jnp.zeros((8, ROWS), jnp.float32)
            centre = jnp.zeros((8, ROWS), jnp.float32)
            step = 64
            for begin in range(0, SPAN * ROWS, step):
                at = slice(begin, begin + step)
                raised = jnp.exp2((s_buf[at] - peak) * (SCALE * LOG2E))
                s_buf[at] = raised
                total = total + fold(jnp.add, raised)
                centre = centre + fold(jnp.add, raised * g_buf[at])
            scale = 1.0 / jnp.sum(total, axis=0, keepdims=True)
            centre = jnp.sum(centre, axis=0, keepdims=True) * scale
            for begin in range(0, SPAN * ROWS, step):
                at = slice(begin, begin + step)
                prob = s_buf[at] * scale
                p_low[at] = prob.astype(jnp.bfloat16)
                s_low[at] = (prob * (g_buf[at] - centre)).astype(jnp.bfloat16)
            nn = (((1,), (0,)), ((), ()))
            key_part = lax.dot_general(s_low[...], query, nn, preferred_element_type=jnp.float32)
            value_part = lax.dot_general(p_low[...], grad, nn, preferred_element_type=jnp.float32)
            for c in range(SPAN):
                at = slice(c * ROWS, (c + 1) * ROWS)
                dkv[j, r + c, :, 0:HEAD_DIM] += key_part[at]
                dkv[j, r + c, :, HEAD_DIM:] += value_part[at]
            query_part = lax.dot_general(
                s_low[...], keys, (((0,), (0,)), ((), ())), preferred_element_type=jnp.float32
            )
            dq_low[j, r, :, hh * HEAD_DIM : (hh + 1) * HEAD_DIM] = (query_part * SCALE).astype(jnp.bfloat16)

    def give(src, dst, n, owner):
        @pl.when(owner == h)
        def _():
            pltpu.make_async_copy(src, dst, own_sem.at[n]).start()

        @pl.when(owner != h)
        def _():
            push(src, dst, out_send.at[n], out_recv.at[n], (s, owner))

    def give_query(j, r):
        col = pl.multiple_of((h * HEADS_KV + j) * PAIR, PAIR)
        for piece in range(2):
            half = slice(piece * (ROWS // 2), (piece + 1) * (ROWS // 2))
            give(dq_low.at[j, r, half], dq_hbm.at[half, pl.ds(col, PAIR)], 0, r)

    def give_kv(j, r):
        col = pl.multiple_of((h * HEADS_KV + j) * HEAD_DIM, HEAD_DIM)
        give(dkv_low.at[j, HALO + r, :, 0:HEAD_DIM], dk_hbm.at[:, pl.ds(col, HEAD_DIM)], 1, r)
        give(dkv_low.at[j, HALO + r, :, HEAD_DIM:], dv_hbm.at[:, pl.ds(col, HEAD_DIM)], 2, r)

    def rounded(j, b, extra=None):
        key_grad = dkv[j, b, :, 0:HEAD_DIM] * SCALE
        value_grad = dkv[j, b, :, HEAD_DIM:]
        if extra is not None:
            key_grad = key_grad + halo_in[j, extra, :, 0:HEAD_DIM].astype(jnp.float32)
            value_grad = value_grad + halo_in[j, extra, :, HEAD_DIM:].astype(jnp.float32)
        dkv_low[j, b, :, 0:HEAD_DIM] = key_grad.astype(jnp.bfloat16)
        dkv_low[j, b, :, HEAD_DIM:] = value_grad.astype(jnp.bfloat16)

    def finish_near(j):
        def one(n, carry):
            r = lax.rem(h + n, HALO)
            rounded(j, HALO + r)
            give_kv(j, r)
            return carry

        lax.fori_loop(0, HALO, one, 0)

    def finish_far(j):
        got(halo_in.at[j], back_recv.at[j])

        def one(n, carry):
            r = lax.rem(h + n, HALO)
            rounded(j, 2 * HALO + r, r)
            give_kv(j, HALO + r)
            return carry

        lax.fori_loop(0, HALO, one, 0)

    for j in range(HEADS_KV):
        got(kv.at[j, 0:HALO], halo_recv.at[j])
        for part in range(2):

            def one(n, carry):
                r = part * HALO + lax.rem(h + n, HALO)
                got(qg.at[j, r], qg_sem.at[j, r])
                unit(j, r)
                give_query(j, r)
                return carry

            lax.fori_loop(0, HALO, one, 0)
            if part == 0:

                def back(b, carry):
                    rounded(j, b)
                    push(dkv_low.at[j, b], halo_in.at[j, b], back_send.at[j], back_recv.at[j], before)
                    return carry

                lax.fori_loop(0, HALO, back, 0)
                if j > 0:
                    finish_far(j - 1)
        finish_near(j)
    finish_far(HEADS_KV - 1)

    for n in range(len(PEERS)):
        got(q_hbm.at[:, 0:1536], in_send.at[n])
    for j in range(HEADS_KV):
        got(kv.at[j, 0:HALO], halo_send.at[j])
        got(halo_in.at[j], back_send.at[j])
    for n, ref in enumerate((dq_hbm, dk_hbm, dv_hbm)):
        wide = ref.shape[1] // 8
        got(ref.at[:, 0:wide], own_sem.at[n])
        got(ref.at[:, 0 : 7 * wide], out_send.at[n])
        got(ref.at[:, 0 : 7 * wide], out_recv.at[n])


def local(queries, key_rows, value_rows, output_grad):
    anywhere = pl.BlockSpec(memory_space=pl.ANY)
    dma = pltpu.SemaphoreType.DMA
    blocks = 8 + HALO
    wide = SPAN * ROWS
    return pl.pallas_call(
        functools.partial(kernel, lax.axis_size("seq")),
        out_shape=[jax.ShapeDtypeStruct(a.shape, a.dtype) for a in (queries, key_rows, value_rows)],
        in_specs=[anywhere] * 4,
        out_specs=[anywhere] * 3,
        scratch_shapes=[
            pltpu.VMEM((HEADS_KV, 8, ROWS, 2 * PAIR), jnp.bfloat16),
            pltpu.VMEM((HEADS_KV, blocks, ROWS, 2 * HEAD_DIM), jnp.bfloat16),
            pltpu.VMEM((HEADS_KV, blocks, ROWS, 2 * HEAD_DIM), jnp.float32),
            pltpu.VMEM((HEADS_KV, blocks, ROWS, 2 * HEAD_DIM), jnp.bfloat16),
            pltpu.VMEM((HEADS_KV, HALO, ROWS, 2 * HEAD_DIM), jnp.bfloat16),
            pltpu.VMEM((HEADS_KV, 8, ROWS, PAIR), jnp.bfloat16),
            pltpu.VMEM((wide, ROWS), jnp.float32),
            pltpu.VMEM((wide, ROWS), jnp.float32),
            pltpu.VMEM((wide, ROWS), jnp.bfloat16),
            pltpu.VMEM((wide, ROWS), jnp.bfloat16),
            dma((HEADS_KV, 8)),
            dma((HEADS_KV, 8)),
            dma((len(PEERS),)),
            dma((HEADS_KV,)),
            dma((HEADS_KV,)),
            dma((HEADS_KV,)),
            dma((HEADS_KV,)),
            dma((3,)),
            dma((3,)),
            dma((3,)),
        ],
        compiler_params=pltpu.CompilerParams(
            collective_id=0, has_side_effects=True, vmem_limit_bytes=60 * 2**20
        ),
        name="window_grads",
    )(queries, key_rows, value_rows, output_grad)


def solution(mesh):
    placed = P(("seq", "head"), None)
    return jax.shard_map(
        local, mesh=mesh, in_specs=(placed,) * 4, out_specs=(placed,) * 3, check_vma=False
    )
```

```python
import functools
import math

import jax
import jax.numpy as jnp
from jax import lax
from jax.experimental import pallas as pl
from jax.experimental.pallas import tpu as pltpu
from jax.sharding import PartitionSpec as P

HEAD_DIM = 128
WINDOW = 1024
GROUP = 2
SCALE = 168.0 ** (-0.5)
LOG2E = math.log2(math.e)
NEG = -1e30

ROWS = 256
HALO = WINDOW // ROWS
SPAN = HALO + 1
ALONG = 4
BLOCKS = 8
HEADS_KV = 4
PAIR = GROUP * HEAD_DIM
MESH = pl.DeviceIdType.MESH
STEPS = (2, 1, 3)


def fold(op, value):
    out = value[0:8]
    for begin in range(8, value.shape[0], 8):
        out = op(out, value[begin : begin + 8])
    return out


def kernel(
    seq_count,
    q_hbm,
    k_hbm,
    v_hbm,
    g_hbm,
    dq_hbm,
    dk_hbm,
    dv_hbm,
    qg,
    kv,
    dkv,
    dkv_low,
    back_in,
    part_in,
    dq_low,
    s_buf,
    g_buf,
    p_low,
    s_low,
    qg_sem,
    kv_sem,
    in_send,
    cross_send,
    cross_recv,
    halo_send,
    halo_recv,
    back_send,
    back_recv,
    part_send,
    part_recv,
    out_send,
    out_recv,
    own_sem,
):
    s, h = lax.axis_index("seq"), lax.axis_index("head")
    x, y = h // 2, lax.rem(h, 2)
    core = lax.rem(s, 2)
    mate = s + 1 - 2 * core
    other = lax.rem(s + 2 * core - 1 + seq_count, seq_count)
    others = [(other, x * 2 + half) for half in range(2)]
    peers = [lax.rem(x + dx, ALONG) * 2 + y for dx in STEPS]
    twin = (s, x * 2 + 1 - y)

    barrier = pltpu.get_barrier_semaphore()
    met = [(s, peer) for peer in peers] + [twin, (mate, h)] + others
    for device in met:
        pl.semaphore_signal(barrier, inc=1, device_id=device, device_id_type=MESH)
    pl.semaphore_wait(barrier, len(met))

    def push(src, dst, send, recv, device):
        pltpu.make_async_remote_copy(
            src_ref=src, dst_ref=dst, send_sem=send, recv_sem=recv, device_id=device, device_id_type=MESH
        ).start()

    def got(ref, sem):
        pltpu.make_async_copy(ref, ref, sem).wait()

    def kv_part(j, owner_x, part):
        col = pl.multiple_of((owner_x * HEADS_KV + j) * HEAD_DIM, HEAD_DIM)
        ref = (k_hbm, v_hbm)[part]
        return ref.at[:, pl.ds(col, HEAD_DIM)], kv.at[j, HALO + h, :, part * HEAD_DIM : (part + 1) * HEAD_DIM]

    def qg_part(j, owner_x, part, piece):
        col = pl.multiple_of((owner_x * HEADS_KV + j) * PAIR, PAIR)
        half = slice(piece * (ROWS // 2), (piece + 1) * (ROWS // 2))
        ref = (q_hbm, g_hbm)[part]
        return ref.at[half, pl.ds(col, PAIR)], qg.at[j, x, half, part * PAIR : (part + 1) * PAIR]

    def push_kv(j):
        for part in range(2):
            for n, peer in enumerate(peers):
                src, dst = kv_part(j, peer // 2, part)
                push(src, dst, in_send.at[n], kv_sem.at[j, x], (s, peer))

    def push_qg(j):
        for piece in range(2):
            for part in range(2):
                for n, peer in enumerate(peers):
                    src, dst = qg_part(j, peer // 2, part, piece)
                    push(src, dst, in_send.at[n], qg_sem.at[j, x], (s, peer))

    push_kv(0)
    push_kv(1)
    push_qg(0)
    push_kv(2)
    push_qg(1)
    push_kv(3)
    push_qg(2)
    push_qg(3)

    def take_own(j, carry):
        for part in range(2):
            src, dst = kv_part(j, x, part)
            pltpu.make_async_copy(src, dst, kv_sem.at[j, x]).start()
            for piece in range(2):
                src, dst = qg_part(j, x, part, piece)
                pltpu.make_async_copy(src, dst, qg_sem.at[j, x]).start()
        return carry

    lax.fori_loop(0, HEADS_KV, take_own, 0)

    def clear(b, carry):
        for j in range(HEADS_KV):
            dkv[j, b] = jnp.zeros((ROWS, 2 * HEAD_DIM), jnp.float32)
        return carry

    lax.fori_loop(0, BLOCKS + HALO, clear, 0)

    def spread_kv(j):
        for i in range(ALONG):
            got(kv.at[j, HALO + 2 * i + y], kv_sem.at[j, i])
        for i in range(ALONG):
            block = kv.at[j, HALO + 2 * i + y]
            push(block, block, cross_send.at[j], cross_recv.at[j], twin)

        @pl.when(core == 1)
        def _():
            for i in range(2):
                for device in others:
                    push(
                        kv.at[j, BLOCKS + 2 * i + y],
                        kv.at[j, 2 * i + y],
                        halo_send.at[j],
                        halo_recv.at[j],
                        device,
                    )

    def halo_on_chip(j):
        got(kv.at[j, 0:ALONG], cross_recv.at[j])

        @pl.when(core == 0)
        def _():
            for b in range(HALO):
                push(kv.at[j, BLOCKS + b], kv.at[j, b], halo_send.at[j], halo_recv.at[j], (mate, h))

    key_row = lax.broadcasted_iota(jnp.int32, (ROWS, ROWS), 0)
    query_col = lax.broadcasted_iota(jnp.int32, (ROWS, ROWS), 1)

    def unit(j, i):
        r = 2 * i + y
        keys = kv[j, pl.ds(r, SPAN), :, 0:HEAD_DIM].reshape(SPAN * ROWS, HEAD_DIM)
        values = kv[j, pl.ds(r, SPAN), :, HEAD_DIM:].reshape(SPAN * ROWS, HEAD_DIM)
        for hh in range(GROUP):
            query = qg[j, i, :, hh * HEAD_DIM : (hh + 1) * HEAD_DIM]
            grad = qg[j, i, :, PAIR + hh * HEAD_DIM : PAIR + (hh + 1) * HEAD_DIM]
            nt = (((1,), (1,)), ((), ()))
            s_buf[...] = lax.dot_general(keys, query, nt, preferred_element_type=jnp.float32)
            g_buf[...] = lax.dot_general(values, grad, nt, preferred_element_type=jnp.float32)
            peak = jnp.full((8, ROWS), NEG, jnp.float32)
            for c in range(SPAN):
                part = s_buf[c * ROWS : (c + 1) * ROWS]
                if c < HALO:
                    inside = (s > 0) | (r + c >= HALO)
                    if c == 0:
                        part = jnp.where((key_row > query_col) & inside, part, NEG)
                    else:
                        part = jnp.where(inside, part, NEG)
                else:
                    part = jnp.where(key_row <= query_col, part, NEG)
                s_buf[c * ROWS : (c + 1) * ROWS] = part
                peak = jnp.maximum(peak, fold(jnp.maximum, part))
            peak = jnp.max(peak, axis=0, keepdims=True)
            total = jnp.zeros((8, ROWS), jnp.float32)
            centre = jnp.zeros((8, ROWS), jnp.float32)
            step = 64
            for begin in range(0, SPAN * ROWS, step):
                at = slice(begin, begin + step)
                raised = jnp.exp2((s_buf[at] - peak) * (SCALE * LOG2E))
                s_buf[at] = raised
                total = total + fold(jnp.add, raised)
                centre = centre + fold(jnp.add, raised * g_buf[at])
            scale = 1.0 / jnp.sum(total, axis=0, keepdims=True)
            centre = jnp.sum(centre, axis=0, keepdims=True) * scale
            for begin in range(0, SPAN * ROWS, step):
                at = slice(begin, begin + step)
                prob = s_buf[at] * scale
                p_low[at] = prob.astype(jnp.bfloat16)
                s_low[at] = (prob * (g_buf[at] - centre)).astype(jnp.bfloat16)
            nn = (((1,), (0,)), ((), ()))
            key_part = lax.dot_general(s_low[...], query, nn, preferred_element_type=jnp.float32)
            value_part = lax.dot_general(p_low[...], grad, nn, preferred_element_type=jnp.float32)
            for c in range(SPAN):
                at = slice(c * ROWS, (c + 1) * ROWS)
                dkv[j, r + c, :, 0:HEAD_DIM] += key_part[at]
                dkv[j, r + c, :, HEAD_DIM:] += value_part[at]
            query_part = lax.dot_general(
                s_low[...], keys, (((0,), (0,)), ((), ())), preferred_element_type=jnp.float32
            )
            dq_low[j, i, :, hh * HEAD_DIM : (hh + 1) * HEAD_DIM] = (query_part * SCALE).astype(jnp.bfloat16)

    def rounded(j, b, extras=()):
        key_grad = dkv[j, b, :, 0:HEAD_DIM] * SCALE
        value_grad = dkv[j, b, :, HEAD_DIM:]
        for extra in extras:
            key_grad = key_grad + extra[:, 0:HEAD_DIM].astype(jnp.float32)
            value_grad = value_grad + extra[:, HEAD_DIM:].astype(jnp.float32)
        dkv_low[j, b, :, 0:HEAD_DIM] = key_grad.astype(jnp.bfloat16)
        dkv_low[j, b, :, HEAD_DIM:] = value_grad.astype(jnp.bfloat16)

    def give_back(j):
        def one(b, carry):
            rounded(j, b)
            block = dkv_low.at[j, b]

            @pl.when(core == 1)
            def _():
                push(block, back_in.at[j, b], back_send.at[j], back_recv.at[j], (mate, h))

            @pl.when(core == 0)
            def _():
                slot = 2 * y + b // 2
                to = (other, x * 2 + lax.rem(b, 2))
                push(block, back_in.at[j, slot], back_send.at[j], back_recv.at[j], to)

            return carry

        lax.fori_loop(0, HALO, one, 0)

    def give_twin(j):
        def send(i, extras=()):
            b = HALO + 2 * i + 1 - y
            rounded(j, b, extras)
            push(dkv_low.at[j, b], part_in.at[j, i], part_send.at[j], part_recv.at[j], twin)

        def near(i, carry):
            send(i)
            return carry

        lax.fori_loop(0, 2, near, 0)
        got(back_in.at[j], back_recv.at[j])

        def far(i, carry):
            @pl.when(core == 0)
            def _():
                send(i, (back_in[j, 2 * i + 1 - y - HALO],))

            @pl.when(core == 1)
            def _():
                send(i)

            return carry

        lax.fori_loop(2, ALONG, far, 0)

    def give(src, dst, n, owner_x):
        @pl.when(owner_x == x)
        def _():
            pltpu.make_async_copy(src, dst, own_sem.at[n]).start()

        @pl.when(owner_x != x)
        def _():
            push(src, dst, out_send.at[n], out_recv.at[n], (s, owner_x * 2 + y))

    def give_query(j):
        col = pl.multiple_of((x * HEADS_KV + j) * PAIR, PAIR)
        for piece in range(2):
            half = slice(piece * (ROWS // 2), (piece + 1) * (ROWS // 2))
            for dx in STEPS + (0,):
                i = lax.rem(x + dx, ALONG)
                give(dq_low.at[j, i, half], dq_hbm.at[half, pl.ds(col, PAIR)], 0, i)

    def give_kv(j):
        got(part_in.at[j], part_recv.at[j])

        def one(i, carry):
            b = HALO + 2 * i + y

            @pl.when(i < 2)
            def _():
                rounded(j, b, (part_in[j, i],))

            @pl.when((i >= 2) & (core == 0))
            def _():
                rounded(j, b, (part_in[j, i], back_in[j, lax.rem(2 * i + y, HALO)]))

            @pl.when((i >= 2) & (core == 1))
            def _():
                slot = lax.rem(i, 2)
                rounded(j, b, (part_in[j, i], back_in[j, slot], back_in[j, 2 + slot]))

            return carry

        lax.fori_loop(0, ALONG, one, 0)
        col = pl.multiple_of((x * HEADS_KV + j) * HEAD_DIM, HEAD_DIM)
        for n, ref in ((1, dk_hbm), (2, dv_hbm)):
            for dx in STEPS + (0,):
                i = lax.rem(x + dx, ALONG)
                at = slice((n - 1) * HEAD_DIM, n * HEAD_DIM)
                give(dkv_low.at[j, HALO + 2 * i + y, :, at], ref.at[:, pl.ds(col, HEAD_DIM)], n, i)

    spread_kv(0)
    spread_kv(1)
    halo_on_chip(0)

    def head(j, carry):
        got(kv.at[j, 0:HALO], halo_recv.at[j])
        for i in range(ALONG):
            got(qg.at[j, i], qg_sem.at[j, i])

        def half(part, carry):
            def one(n, carry):
                unit(j, 2 * part + lax.rem(x + n, 2))
                return carry

            lax.fori_loop(0, 2, one, 0)

            @pl.when(part == 0)
            def _():
                give_back(j)

                @pl.when(j + 2 < HEADS_KV)
                def _():
                    spread_kv(j + 2)

                @pl.when(j + 1 < HEADS_KV)
                def _():
                    halo_on_chip(j + 1)

                @pl.when(j >= 1)
                def _():
                    give_kv(j - 1)

            return carry

        lax.fori_loop(0, 2, half, 0)
        give_query(j)
        give_twin(j)
        return carry

    lax.fori_loop(0, HEADS_KV, head, 0)
    give_kv(HEADS_KV - 1)

    for n in range(len(STEPS)):
        got(q_hbm.at[:, 0:3072], in_send.at[n])
    for j in range(HEADS_KV):
        for sem in (cross_send, halo_send, back_send, part_send):
            got(back_in.at[j], sem.at[j])
    for n, ref in enumerate((dq_hbm, dk_hbm, dv_hbm)):
        wide = ref.shape[1] // ALONG
        got(ref.at[:, 0:wide], own_sem.at[n])
        got(ref.at[:, 0 : 3 * wide], out_send.at[n])
        got(ref.at[:, 0 : 3 * wide], out_recv.at[n])


def local(queries, key_rows, value_rows, output_grad):
    anywhere = pl.BlockSpec(memory_space=pl.ANY)
    dma = pltpu.SemaphoreType.DMA
    blocks = BLOCKS + HALO
    wide = SPAN * ROWS
    return pl.pallas_call(
        functools.partial(kernel, lax.axis_size("seq")),
        out_shape=[jax.ShapeDtypeStruct(a.shape, a.dtype) for a in (queries, key_rows, value_rows)],
        in_specs=[anywhere] * 4,
        out_specs=[anywhere] * 3,
        scratch_shapes=[
            pltpu.VMEM((HEADS_KV, ALONG, ROWS, 2 * PAIR), jnp.bfloat16),
            pltpu.VMEM((HEADS_KV, blocks, ROWS, 2 * HEAD_DIM), jnp.bfloat16),
            pltpu.VMEM((HEADS_KV, blocks, ROWS, 2 * HEAD_DIM), jnp.float32),
            pltpu.VMEM((HEADS_KV, blocks, ROWS, 2 * HEAD_DIM), jnp.bfloat16),
            pltpu.VMEM((HEADS_KV, HALO, ROWS, 2 * HEAD_DIM), jnp.bfloat16),
            pltpu.VMEM((HEADS_KV, ALONG, ROWS, 2 * HEAD_DIM), jnp.bfloat16),
            pltpu.VMEM((HEADS_KV, ALONG, ROWS, PAIR), jnp.bfloat16),
            pltpu.VMEM((wide, ROWS), jnp.float32),
            pltpu.VMEM((wide, ROWS), jnp.float32),
            pltpu.VMEM((wide, ROWS), jnp.bfloat16),
            pltpu.VMEM((wide, ROWS), jnp.bfloat16),
            dma((HEADS_KV, ALONG)),
            dma((HEADS_KV, ALONG)),
            dma((len(STEPS),)),
            *[dma((HEADS_KV,)) for _ in range(8)],
            dma((3,)),
            dma((3,)),
            dma((3,)),
        ],
        compiler_params=pltpu.CompilerParams(
            collective_id=0, has_side_effects=True, vmem_limit_bytes=60 * 2**20
        ),
        name="window_grads",
    )(queries, key_rows, value_rows, output_grad)


def solution(mesh):
    placed = P(("seq", "head"), None)
    return jax.shard_map(
        local, mesh=mesh, in_specs=(placed,) * 4, out_specs=(placed,) * 3, check_vma=False
    )
```

```python
import functools
import math

import jax
import jax.numpy as jnp
from jax import lax
from jax.experimental import pallas as pl
from jax.experimental.pallas import tpu as pltpu
from jax.sharding import PartitionSpec as P

HEAD_DIM = 128
WINDOW = 1024
GROUP = 2
SCALE = 168.0 ** (-0.5)
LOG2E = math.log2(math.e)
NEG = -1e30

ROWS = 256
HALO = WINDOW // ROWS
SPAN = HALO + 1
ALONG = 4
BLOCKS = 8
HEADS_KV = 4
PAIR = GROUP * HEAD_DIM
MESH = pl.DeviceIdType.MESH
STEPS = (2, 1, 3)


def fold(op, value):
    out = value[0:8]
    for begin in range(8, value.shape[0], 8):
        out = op(out, value[begin : begin + 8])
    return out


def kernel(
    seq_count,
    q_hbm,
    k_hbm,
    v_hbm,
    g_hbm,
    dq_hbm,
    dk_hbm,
    dv_hbm,
    qg,
    kv,
    dkv,
    dkv_low,
    back_in,
    part_in,
    dq_low,
    s_buf,
    g_buf,
    p_low,
    s_low,
    qg_sem,
    kv_sem,
    in_send,
    cross_send,
    cross_recv,
    halo_send,
    halo_recv,
    back_send,
    back_recv,
    part_send,
    part_recv,
    out_send,
    out_recv,
    own_sem,
):
    s, h = lax.axis_index("seq"), lax.axis_index("head")
    x, y = h // 2, lax.rem(h, 2)
    core = lax.rem(s, 2)
    mate = s + 1 - 2 * core
    other = lax.rem(s + 2 * core - 1 + seq_count, seq_count)
    others = [(other, x * 2 + half) for half in range(2)]
    peers = [lax.rem(x + dx, ALONG) * 2 + y for dx in STEPS]
    twin = (s, x * 2 + 1 - y)

    barrier = pltpu.get_barrier_semaphore()
    met = [(s, peer) for peer in peers] + [twin, (mate, h)] + others
    for device in met:
        pl.semaphore_signal(barrier, inc=1, device_id=device, device_id_type=MESH)
    pl.semaphore_wait(barrier, len(met))

    def push(src, dst, send, recv, device):
        pltpu.make_async_remote_copy(
            src_ref=src, dst_ref=dst, send_sem=send, recv_sem=recv, device_id=device, device_id_type=MESH
        ).start()

    def got(ref, sem):
        pltpu.make_async_copy(ref, ref, sem).wait()

    def got_blocks(ref, sem, fewer):
        @pl.when(fewer)
        def _():
            got(ref.at[1:4], sem)

        @pl.when(jnp.logical_not(fewer))
        def _():
            got(ref.at[0:4], sem)

    def cross_has(i, half):
        return (i < ALONG - 1) | (half == 0) | (core == 0)

    def kv_part(j, owner_x, part):
        col = pl.multiple_of((owner_x * HEADS_KV + j) * HEAD_DIM, HEAD_DIM)
        ref = (k_hbm, v_hbm)[part]
        return ref.at[:, pl.ds(col, HEAD_DIM)], kv.at[j, HALO + h, :, part * HEAD_DIM : (part + 1) * HEAD_DIM]

    def qg_part(j, owner_x, part, piece):
        col = pl.multiple_of((owner_x * HEADS_KV + j) * PAIR, PAIR)
        half = slice(piece * (ROWS // 2), (piece + 1) * (ROWS // 2))
        ref = (q_hbm, g_hbm)[part]
        return ref.at[half, pl.ds(col, PAIR)], qg.at[j, x, half, part * PAIR : (part + 1) * PAIR]

    def push_kv(j):
        for part in range(2):
            for n, peer in enumerate(peers):
                src, dst = kv_part(j, peer // 2, part)
                push(src, dst, in_send.at[n], kv_sem.at[j, x], (s, peer))

    def push_qg(j):
        for piece in range(2):
            for part in range(2):
                for n, peer in enumerate(peers):
                    src, dst = qg_part(j, peer // 2, part, piece)
                    push(src, dst, in_send.at[n], qg_sem.at[j, x], (s, peer))

    push_kv(0)
    for j in range(HEADS_KV):

        @pl.when(cross_has(x, y))
        def _(j=j):
            for part in range(2):
                src, dst = kv_part(j, x, part)
                push(src, dst, cross_send.at[j], cross_recv.at[j], twin)

    push_kv(1)
    push_qg(0)
    push_kv(2)
    push_qg(1)
    push_kv(3)
    push_qg(2)
    push_qg(3)

    def take_own(j, carry):
        for part in range(2):
            src, dst = kv_part(j, x, part)
            pltpu.make_async_copy(src, dst, kv_sem.at[j, x]).start()
            for piece in range(2):
                src, dst = qg_part(j, x, part, piece)
                pltpu.make_async_copy(src, dst, qg_sem.at[j, x]).start()
        return carry

    lax.fori_loop(0, HEADS_KV, take_own, 0)

    def clear(b, carry):
        for j in range(HEADS_KV):
            dkv[j, b] = jnp.zeros((ROWS, 2 * HEAD_DIM), jnp.float32)
        return carry

    lax.fori_loop(0, BLOCKS + HALO, clear, 0)

    def spread_kv(j):
        for i in range(ALONG):
            got(kv.at[j, HALO + 2 * i + y], kv_sem.at[j, i])
        for dx in STEPS:
            i = lax.rem(x + dx, ALONG)

            @pl.when(cross_has(i, y))
            def _(i=i):
                block = kv.at[j, HALO + 2 * i + y]
                push(block, block, cross_send.at[j], cross_recv.at[j], twin)

        def send_halo(i, half):
            src, dst = kv.at[j, BLOCKS + 2 * i + y], kv.at[j, 2 * i + y]
            push(src, dst, halo_send.at[j], halo_recv.at[j], others[half])

        @pl.when(core == 1)
        def _():
            for i in range(2):
                send_halo(i, 0)
            send_halo(1, 1)

            @pl.when(y == 1)
            def _():
                send_halo(0, 1)

    def halo_on_chip(j):
        got_blocks(kv.at[j], cross_recv.at[j], (core == 1) & (y == 0))

        @pl.when(core == 0)
        def _():
            for b in range(HALO):
                push(kv.at[j, BLOCKS + b], kv.at[j, b], halo_send.at[j], halo_recv.at[j], (mate, h))

    key_row = lax.broadcasted_iota(jnp.int32, (ROWS, ROWS), 0)
    query_col = lax.broadcasted_iota(jnp.int32, (ROWS, ROWS), 1)

    def unit(j, i):
        r = 2 * i + y
        keys = kv[j, pl.ds(r, SPAN), :, 0:HEAD_DIM].reshape(SPAN * ROWS, HEAD_DIM)
        values = kv[j, pl.ds(r, SPAN), :, HEAD_DIM:].reshape(SPAN * ROWS, HEAD_DIM)
        for hh in range(GROUP):
            query = qg[j, i, :, hh * HEAD_DIM : (hh + 1) * HEAD_DIM]
            grad = qg[j, i, :, PAIR + hh * HEAD_DIM : PAIR + (hh + 1) * HEAD_DIM]
            nt = (((1,), (1,)), ((), ()))
            s_buf[...] = lax.dot_general(keys, query, nt, preferred_element_type=jnp.float32)
            g_buf[...] = lax.dot_general(values, grad, nt, preferred_element_type=jnp.float32)
            peak = jnp.full((8, ROWS), NEG, jnp.float32)
            for c in range(SPAN):
                part = s_buf[c * ROWS : (c + 1) * ROWS]
                if c < HALO:
                    inside = (s > 0) | (r + c >= HALO)
                    if c == 0:
                        part = jnp.where((key_row > query_col) & inside, part, NEG)
                    else:
                        part = jnp.where(inside, part, NEG)
                else:
                    part = jnp.where(key_row <= query_col, part, NEG)
                s_buf[c * ROWS : (c + 1) * ROWS] = part
                peak = jnp.maximum(peak, fold(jnp.maximum, part))
            peak = jnp.max(peak, axis=0, keepdims=True)
            total = jnp.zeros((8, ROWS), jnp.float32)
            centre = jnp.zeros((8, ROWS), jnp.float32)
            step = 64
            for begin in range(0, SPAN * ROWS, step):
                at = slice(begin, begin + step)
                raised = jnp.exp2((s_buf[at] - peak) * (SCALE * LOG2E))
                s_buf[at] = raised
                total = total + fold(jnp.add, raised)
                centre = centre + fold(jnp.add, raised * g_buf[at])
            scale = 1.0 / jnp.sum(total, axis=0, keepdims=True)
            centre = jnp.sum(centre, axis=0, keepdims=True) * scale
            for begin in range(0, SPAN * ROWS, step):
                at = slice(begin, begin + step)
                prob = s_buf[at] * scale
                p_low[at] = prob.astype(jnp.bfloat16)
                s_low[at] = (prob * (g_buf[at] - centre)).astype(jnp.bfloat16)
            nn = (((1,), (0,)), ((), ()))
            key_part = lax.dot_general(s_low[...], query, nn, preferred_element_type=jnp.float32)
            value_part = lax.dot_general(p_low[...], grad, nn, preferred_element_type=jnp.float32)
            for c in range(SPAN):
                at = slice(c * ROWS, (c + 1) * ROWS)
                dkv[j, r + c, :, 0:HEAD_DIM] += key_part[at]
                dkv[j, r + c, :, HEAD_DIM:] += value_part[at]
            query_part = lax.dot_general(
                s_low[...], keys, (((0,), (0,)), ((), ())), preferred_element_type=jnp.float32
            )
            dq_low[j, i, :, hh * HEAD_DIM : (hh + 1) * HEAD_DIM] = (query_part * SCALE).astype(jnp.bfloat16)

    def rounded(j, b, extras=()):
        key_grad = dkv[j, b, :, 0:HEAD_DIM] * SCALE
        value_grad = dkv[j, b, :, HEAD_DIM:]
        for extra in extras:
            key_grad = key_grad + extra[:, 0:HEAD_DIM].astype(jnp.float32)
            value_grad = value_grad + extra[:, HEAD_DIM:].astype(jnp.float32)
        dkv_low[j, b, :, 0:HEAD_DIM] = key_grad.astype(jnp.bfloat16)
        dkv_low[j, b, :, HEAD_DIM:] = value_grad.astype(jnp.bfloat16)

    def give_back(j):
        def one(b, carry):
            rounded(j, b)
            block = dkv_low.at[j, b]

            @pl.when(core == 1)
            def _():
                push(block, back_in.at[j, b], back_send.at[j], back_recv.at[j], (mate, h))

            @pl.when((core == 0) & (b >= y))
            def _():
                slot = 2 * y + b // 2
                to = (other, x * 2 + lax.rem(b, 2))
                push(block, back_in.at[j, slot], back_send.at[j], back_recv.at[j], to)

            return carry

        lax.fori_loop(0, HALO, one, 0)

    def give_twin(j):
        got_blocks(back_in.at[j], back_recv.at[j], (core == 1) & (y == 0))

        def one(n, carry):
            i = lax.rem(x + jnp.where(n == 0, 2, jnp.where(n == 1, 1, jnp.where(n == 2, 3, 0))), ALONG)
            b = HALO + 2 * i + 1 - y

            @pl.when((core == 0) & (i >= 2))
            def _():
                rounded(j, b, (back_in[j, lax.rem(2 * i + 1 - y, HALO)],))

            @pl.when((core == 1) | (i < 2))
            def _():
                rounded(j, b)

            @pl.when(cross_has(i, 1 - y))
            def _():
                push(dkv_low.at[j, b], part_in.at[j, i], part_send.at[j], part_recv.at[j, i], twin)

            return carry

        lax.fori_loop(0, ALONG, one, 0)

    def give(src, dst, n, owner_x):
        @pl.when(owner_x == x)
        def _():
            pltpu.make_async_copy(src, dst, own_sem.at[n]).start()

        @pl.when(owner_x != x)
        def _():
            push(src, dst, out_send.at[n], out_recv.at[n], (s, owner_x * 2 + y))

    def give_query(j):
        col = pl.multiple_of((x * HEADS_KV + j) * PAIR, PAIR)
        for piece in range(2):
            half = slice(piece * (ROWS // 2), (piece + 1) * (ROWS // 2))
            for dx in STEPS + (0,):
                i = lax.rem(x + dx, ALONG)
                give(dq_low.at[j, i, half], dq_hbm.at[half, pl.ds(col, PAIR)], 0, i)

    def give_kv(j):
        col = pl.multiple_of((x * HEADS_KV + j) * HEAD_DIM, HEAD_DIM)

        def one(n, carry):
            i = lax.rem(x + jnp.where(n == 0, 2, jnp.where(n == 1, 1, jnp.where(n == 2, 3, 0))), ALONG)
            b = HALO + 2 * i + y
            slot = lax.rem(i, 2)

            @pl.when(cross_has(i, y))
            def _():
                got(part_in.at[j, i], part_recv.at[j, i])

            @pl.when(i < 2)
            def _():
                rounded(j, b, (part_in[j, i],))

            @pl.when((i >= 2) & (core == 0))
            def _():
                rounded(j, b, (part_in[j, i], back_in[j, lax.rem(2 * i + y, HALO)]))

            @pl.when((i == 2) & (core == 1) & (y == 0))
            def _():
                rounded(j, b, (part_in[j, i], back_in[j, slot]))

            @pl.when((i == 2) & (core == 1) & (y == 1))
            def _():
                rounded(j, b, (part_in[j, i], back_in[j, slot], back_in[j, 2 + slot]))

            @pl.when((i == 3) & (core == 1) & (y == 0))
            def _():
                rounded(j, b, (part_in[j, i], back_in[j, slot], back_in[j, 2 + slot]))

            @pl.when((i == 3) & (core == 1) & (y == 1))
            def _():
                rounded(j, b, (back_in[j, slot], back_in[j, 2 + slot]))

            give(dkv_low.at[j, b, :, 0:HEAD_DIM], dk_hbm.at[:, pl.ds(col, HEAD_DIM)], 1, i)
            give(dkv_low.at[j, b, :, HEAD_DIM:], dv_hbm.at[:, pl.ds(col, HEAD_DIM)], 2, i)
            return carry

        lax.fori_loop(0, ALONG, one, 0)

    spread_kv(0)
    spread_kv(1)
    halo_on_chip(0)

    def head(j, carry):
        got_blocks(kv.at[j], halo_recv.at[j], (core == 0) & (y == 1))
        for i in range(ALONG):
            got(qg.at[j, i], qg_sem.at[j, i])

        def half(part, carry):
            def one(n, carry):
                unit(j, 2 * part + lax.rem(x + n, 2))
                return carry

            lax.fori_loop(0, 2, one, 0)

            @pl.when(part == 0)
            def _():
                give_back(j)

                @pl.when(j + 2 < HEADS_KV)
                def _():
                    spread_kv(j + 2)

                @pl.when(j + 1 < HEADS_KV)
                def _():
                    halo_on_chip(j + 1)

            return carry

        lax.fori_loop(0, 2, half, 0)
        give_query(j)
        give_twin(j)

        @pl.when(j >= 1)
        def _():
            give_kv(j - 1)

        return carry

    lax.fori_loop(0, HEADS_KV, head, 0)
    give_kv(HEADS_KV - 1)

    for n in range(len(STEPS)):
        got(q_hbm.at[:, 0:3072], in_send.at[n])
    for j in range(HEADS_KV):
        got_blocks(back_in.at[j], cross_send.at[j], (core == 1) & (y == 1))
        got_blocks(back_in.at[j], halo_send.at[j], (core == 1) & (y == 0))
        got_blocks(back_in.at[j], back_send.at[j], (core == 0) & (y == 1))
        got_blocks(back_in.at[j], part_send.at[j], (core == 1) & (y == 0))
    for n, ref in enumerate((dq_hbm, dk_hbm, dv_hbm)):
        wide = ref.shape[1] // ALONG
        got(ref.at[:, 0:wide], own_sem.at[n])
        got(ref.at[:, 0 : 3 * wide], out_send.at[n])
        got(ref.at[:, 0 : 3 * wide], out_recv.at[n])


def local(queries, key_rows, value_rows, output_grad):
    anywhere = pl.BlockSpec(memory_space=pl.ANY)
    dma = pltpu.SemaphoreType.DMA
    blocks = BLOCKS + HALO
    wide = SPAN * ROWS
    return pl.pallas_call(
        functools.partial(kernel, lax.axis_size("seq")),
        out_shape=[jax.ShapeDtypeStruct(a.shape, a.dtype) for a in (queries, key_rows, value_rows)],
        in_specs=[anywhere] * 4,
        out_specs=[anywhere] * 3,
        scratch_shapes=[
            pltpu.VMEM((HEADS_KV, ALONG, ROWS, 2 * PAIR), jnp.bfloat16),
            pltpu.VMEM((HEADS_KV, blocks, ROWS, 2 * HEAD_DIM), jnp.bfloat16),
            pltpu.VMEM((HEADS_KV, blocks, ROWS, 2 * HEAD_DIM), jnp.float32),
            pltpu.VMEM((HEADS_KV, blocks, ROWS, 2 * HEAD_DIM), jnp.bfloat16),
            pltpu.VMEM((HEADS_KV, HALO, ROWS, 2 * HEAD_DIM), jnp.bfloat16),
            pltpu.VMEM((HEADS_KV, ALONG, ROWS, 2 * HEAD_DIM), jnp.bfloat16),
            pltpu.VMEM((HEADS_KV, ALONG, ROWS, PAIR), jnp.bfloat16),
            pltpu.VMEM((wide, ROWS), jnp.float32),
            pltpu.VMEM((wide, ROWS), jnp.float32),
            pltpu.VMEM((wide, ROWS), jnp.bfloat16),
            pltpu.VMEM((wide, ROWS), jnp.bfloat16),
            dma((HEADS_KV, ALONG)),
            dma((HEADS_KV, ALONG)),
            dma((len(STEPS),)),
            *[dma((HEADS_KV,)) for _ in range(7)],
            dma((HEADS_KV, ALONG)),
            dma((3,)),
            dma((3,)),
            dma((3,)),
        ],
        compiler_params=pltpu.CompilerParams(
            collective_id=0, has_side_effects=True, vmem_limit_bytes=60 * 2**20
        ),
        name="window_grads",
    )(queries, key_rows, value_rows, output_grad)


def solution(mesh):
    placed = P(("seq", "head"), None)
    return jax.shard_map(
        local, mesh=mesh, in_specs=(placed,) * 4, out_specs=(placed,) * 3, check_vma=False
    )
```

```python
import functools
import math

import jax
import jax.numpy as jnp
from jax import lax
from jax.experimental import pallas as pl
from jax.experimental.pallas import tpu as pltpu
from jax.sharding import PartitionSpec as P

HEAD_DIM = 128
WINDOW = 1024
GROUP = 2
SCALE = 168.0 ** (-0.5)
LOG2E = math.log2(math.e)
NEG = -1e30

ROWS = 256
HALO = WINDOW // ROWS
SPAN = HALO + 1
ALONG = 4
BLOCKS = 8
HEADS_KV = 4
PAIR = GROUP * HEAD_DIM
MESH = pl.DeviceIdType.MESH
STEPS = (2, 1, 3)


def fold(op, value):
    out = value[0:8]
    for begin in range(8, value.shape[0], 8):
        out = op(out, value[begin : begin + 8])
    return out


def kernel(
    seq_count,
    q_hbm,
    k_hbm,
    v_hbm,
    g_hbm,
    dq_hbm,
    dk_hbm,
    dv_hbm,
    qg,
    kv,
    dkv,
    dkv_low,
    back_in,
    part_in,
    dq_low,
    s_buf,
    g_buf,
    p_low,
    s_low,
    qg_sem,
    kv_sem,
    in_send,
    cross_send,
    cross_recv,
    halo_send,
    halo_recv,
    back_send,
    back_recv,
    part_send,
    part_recv,
    out_send,
    out_recv,
    own_sem,
):
    s, h = lax.axis_index("seq"), lax.axis_index("head")
    x, y = h // 2, lax.rem(h, 2)
    core = lax.rem(s, 2)
    mate = s + 1 - 2 * core
    other = lax.rem(s + 2 * core - 1 + seq_count, seq_count)
    others = [(other, x * 2 + half) for half in range(2)]
    peers = [lax.rem(x + dx, ALONG) * 2 + y for dx in STEPS]
    twin = (s, x * 2 + 1 - y)

    barrier = pltpu.get_barrier_semaphore()
    met = [(s, peer) for peer in peers] + [twin, (mate, h)] + others
    for device in met:
        pl.semaphore_signal(barrier, inc=1, device_id=device, device_id_type=MESH)
    pl.semaphore_wait(barrier, len(met))

    def push(src, dst, send, recv, device):
        pltpu.make_async_remote_copy(
            src_ref=src, dst_ref=dst, send_sem=send, recv_sem=recv, device_id=device, device_id_type=MESH
        ).start()

    def got(ref, sem):
        pltpu.make_async_copy(ref, ref, sem).wait()

    def got_blocks(ref, sem, fewer):
        @pl.when(fewer)
        def _():
            got(ref.at[1:4], sem)

        @pl.when(jnp.logical_not(fewer))
        def _():
            got(ref.at[0:4], sem)

    def cross_has(i, half):
        return (i < ALONG - 1) | (half == 0) | (core == 0)

    def kv_part(j, owner_x, part):
        col = pl.multiple_of((owner_x * HEADS_KV + j) * HEAD_DIM, HEAD_DIM)
        ref = (k_hbm, v_hbm)[part]
        return ref.at[:, pl.ds(col, HEAD_DIM)], kv.at[j, HALO + h, :, part * HEAD_DIM : (part + 1) * HEAD_DIM]

    def qg_part(j, owner_x, part, piece):
        col = pl.multiple_of((owner_x * HEADS_KV + j) * PAIR, PAIR)
        half = slice(piece * (ROWS // 2), (piece + 1) * (ROWS // 2))
        ref = (q_hbm, g_hbm)[part]
        return ref.at[half, pl.ds(col, PAIR)], qg.at[j, x, half, part * PAIR : (part + 1) * PAIR]

    def push_kv(j):
        for part in range(2):
            for n, peer in enumerate(peers):
                src, dst = kv_part(j, peer // 2, part)
                push(src, dst, in_send.at[n], kv_sem.at[j, x], (s, peer))

    def push_qg(j):
        for piece in range(2):
            for part in range(2):
                for n, peer in enumerate(peers):
                    src, dst = qg_part(j, peer // 2, part, piece)
                    push(src, dst, in_send.at[n], qg_sem.at[j, x], (s, peer))

    push_kv(0)
    for j in range(HEADS_KV):

        @pl.when(cross_has(x, y))
        def _(j=j):
            for part in range(2):
                src, dst = kv_part(j, x, part)
                push(src, dst, cross_send.at[j], cross_recv.at[j], twin)

    push_kv(1)
    push_qg(0)
    push_kv(2)
    push_qg(1)
    push_kv(3)
    push_qg(2)
    push_qg(3)

    def take_own(j, carry):
        for part in range(2):
            src, dst = kv_part(j, x, part)
            pltpu.make_async_copy(src, dst, kv_sem.at[j, x]).start()
            for piece in range(2):
                src, dst = qg_part(j, x, part, piece)
                pltpu.make_async_copy(src, dst, qg_sem.at[j, x]).start()
        return carry

    lax.fori_loop(0, HEADS_KV, take_own, 0)

    def clear(b, carry):
        for j in range(HEADS_KV):
            dkv[j, b] = jnp.zeros((ROWS, 2 * HEAD_DIM), jnp.float32)
        return carry

    lax.fori_loop(0, BLOCKS + HALO, clear, 0)

    def spread_kv(j):
        for i in range(ALONG):
            got(kv.at[j, HALO + 2 * i + y], kv_sem.at[j, i])
        for dx in STEPS:
            i = lax.rem(x + dx, ALONG)

            @pl.when(cross_has(i, y))
            def _(i=i):
                block = kv.at[j, HALO + 2 * i + y]
                push(block, block, cross_send.at[j], cross_recv.at[j], twin)

        def send_halo(i, half):
            src, dst = kv.at[j, BLOCKS + 2 * i + y], kv.at[j, 2 * i + y]
            push(src, dst, halo_send.at[j], halo_recv.at[j], others[half])

        @pl.when(core == 1)
        def _():
            for i in range(2):
                send_halo(i, 0)
            send_halo(1, 1)

            @pl.when(y == 1)
            def _():
                send_halo(0, 1)

    def halo_on_chip(j):
        got_blocks(kv.at[j], cross_recv.at[j], (core == 1) & (y == 0))

        @pl.when(core == 0)
        def _():
            for b in range(HALO):
                push(kv.at[j, BLOCKS + b], kv.at[j, b], halo_send.at[j], halo_recv.at[j], (mate, h))

    key_row = lax.broadcasted_iota(jnp.int32, (ROWS, ROWS), 0)
    query_col = lax.broadcasted_iota(jnp.int32, (ROWS, ROWS), 1)

    def unit(j, i):
        r = 2 * i + y
        keys = kv[j, pl.ds(r, SPAN), :, 0:HEAD_DIM].reshape(SPAN * ROWS, HEAD_DIM)
        values = kv[j, pl.ds(r, SPAN), :, HEAD_DIM:].reshape(SPAN * ROWS, HEAD_DIM)
        for hh in range(GROUP):
            query = qg[j, i, :, hh * HEAD_DIM : (hh + 1) * HEAD_DIM]
            grad = qg[j, i, :, PAIR + hh * HEAD_DIM : PAIR + (hh + 1) * HEAD_DIM]
            nt = (((1,), (1,)), ((), ()))
            s_buf[...] = lax.dot_general(keys, query, nt, preferred_element_type=jnp.float32)
            g_buf[...] = lax.dot_general(values, grad, nt, preferred_element_type=jnp.float32)
            peak = jnp.full((8, ROWS), NEG, jnp.float32)
            for c in range(SPAN):
                part = s_buf[c * ROWS : (c + 1) * ROWS]
                if c < HALO:
                    inside = (s > 0) | (r + c >= HALO)
                    if c == 0:
                        part = jnp.where((key_row > query_col) & inside, part, NEG)
                    else:
                        part = jnp.where(inside, part, NEG)
                else:
                    part = jnp.where(key_row <= query_col, part, NEG)
                s_buf[c * ROWS : (c + 1) * ROWS] = part
                peak = jnp.maximum(peak, fold(jnp.maximum, part))
            peak = jnp.max(peak, axis=0, keepdims=True)
            total = jnp.zeros((8, ROWS), jnp.float32)
            centre = jnp.zeros((8, ROWS), jnp.float32)
            step = 64
            for begin in range(0, SPAN * ROWS, step):
                at = slice(begin, begin + step)
                raised = jnp.exp2((s_buf[at] - peak) * (SCALE * LOG2E))
                s_buf[at] = raised
                total = total + fold(jnp.add, raised)
                centre = centre + fold(jnp.add, raised * g_buf[at])
            scale = 1.0 / jnp.sum(total, axis=0, keepdims=True)
            centre = jnp.sum(centre, axis=0, keepdims=True) * scale
            for begin in range(0, SPAN * ROWS, step):
                at = slice(begin, begin + step)
                prob = s_buf[at] * scale
                p_low[at] = prob.astype(jnp.bfloat16)
                s_low[at] = (prob * (g_buf[at] - centre)).astype(jnp.bfloat16)
            nn = (((1,), (0,)), ((), ()))
            key_part = lax.dot_general(s_low[...], query, nn, preferred_element_type=jnp.float32)
            value_part = lax.dot_general(p_low[...], grad, nn, preferred_element_type=jnp.float32)
            for c in range(SPAN):
                at = slice(c * ROWS, (c + 1) * ROWS)
                dkv[j, r + c, :, 0:HEAD_DIM] += key_part[at]
                dkv[j, r + c, :, HEAD_DIM:] += value_part[at]
            query_part = lax.dot_general(
                s_low[...], keys, (((0,), (0,)), ((), ())), preferred_element_type=jnp.float32
            )
            dq_low[j, i, :, hh * HEAD_DIM : (hh + 1) * HEAD_DIM] = (query_part * SCALE).astype(jnp.bfloat16)

    def rounded(j, b, extras=()):
        key_grad = dkv[j, b, :, 0:HEAD_DIM] * SCALE
        value_grad = dkv[j, b, :, HEAD_DIM:]
        for extra in extras:
            key_grad = key_grad + extra[:, 0:HEAD_DIM].astype(jnp.float32)
            value_grad = value_grad + extra[:, HEAD_DIM:].astype(jnp.float32)
        dkv_low[j, b, :, 0:HEAD_DIM] = key_grad.astype(jnp.bfloat16)
        dkv_low[j, b, :, HEAD_DIM:] = value_grad.astype(jnp.bfloat16)

    def give_back(j):
        def one(b, carry):
            rounded(j, b)
            block = dkv_low.at[j, b]

            @pl.when(core == 1)
            def _():
                push(block, back_in.at[j, b], back_send.at[j], back_recv.at[j], (mate, h))

            @pl.when((core == 0) & (b >= y))
            def _():
                slot = 2 * y + b // 2
                to = (other, x * 2 + lax.rem(b, 2))
                push(block, back_in.at[j, slot], back_send.at[j], back_recv.at[j], to)

            return carry

        lax.fori_loop(0, HALO, one, 0)

    def give_twin(j):
        got_blocks(back_in.at[j], back_recv.at[j], (core == 1) & (y == 0))

        def one(n, carry):
            i = lax.rem(x + jnp.where(n == 0, 2, jnp.where(n == 1, 1, jnp.where(n == 2, 3, 0))), ALONG)
            b = HALO + 2 * i + 1 - y

            @pl.when((core == 0) & (i >= 2))
            def _():
                rounded(j, b, (back_in[j, lax.rem(2 * i + 1 - y, HALO)],))

            @pl.when((core == 1) | (i < 2))
            def _():
                rounded(j, b)

            @pl.when(cross_has(i, 1 - y))
            def _():
                push(dkv_low.at[j, b], part_in.at[j, i], part_send.at[j], part_recv.at[j, i], twin)

            return carry

        lax.fori_loop(0, ALONG, one, 0)

    def give(src, dst, n, owner_x):
        @pl.when(owner_x == x)
        def _():
            pltpu.make_async_copy(src, dst, own_sem.at[n]).start()

        @pl.when(owner_x != x)
        def _():
            push(src, dst, out_send.at[n], out_recv.at[n], (s, owner_x * 2 + y))

    def give_query(j):
        col = pl.multiple_of((x * HEADS_KV + j) * PAIR, PAIR)
        for piece in range(2):
            half = slice(piece * (ROWS // 2), (piece + 1) * (ROWS // 2))
            for dx in STEPS + (0,):
                i = lax.rem(x + dx, ALONG)
                give(dq_low.at[j, i, half], dq_hbm.at[half, pl.ds(col, PAIR)], 0, i)

    def give_kv(j):
        col = pl.multiple_of((x * HEADS_KV + j) * HEAD_DIM, HEAD_DIM)

        def one(n, carry):
            i = lax.rem(x + jnp.where(n == 0, 2, jnp.where(n == 1, 1, jnp.where(n == 2, 3, 0))), ALONG)
            b = HALO + 2 * i + y
            slot = lax.rem(i, 2)

            @pl.when(cross_has(i, y))
            def _():
                got(part_in.at[j, i], part_recv.at[j, i])

            @pl.when(i < 2)
            def _():
                rounded(j, b, (part_in[j, i],))

            @pl.when((i >= 2) & (core == 0))
            def _():
                rounded(j, b, (part_in[j, i], back_in[j, lax.rem(2 * i + y, HALO)]))

            @pl.when((i == 2) & (core == 1) & (y == 0))
            def _():
                rounded(j, b, (part_in[j, i], back_in[j, slot]))

            @pl.when((i == 2) & (core == 1) & (y == 1))
            def _():
                rounded(j, b, (part_in[j, i], back_in[j, slot], back_in[j, 2 + slot]))

            @pl.when((i == 3) & (core == 1) & (y == 0))
            def _():
                rounded(j, b, (part_in[j, i], back_in[j, slot], back_in[j, 2 + slot]))

            @pl.when((i == 3) & (core == 1) & (y == 1))
            def _():
                rounded(j, b, (back_in[j, slot], back_in[j, 2 + slot]))

            give(dkv_low.at[j, b, :, 0:HEAD_DIM], dk_hbm.at[:, pl.ds(col, HEAD_DIM)], 1, i)
            give(dkv_low.at[j, b, :, HEAD_DIM:], dv_hbm.at[:, pl.ds(col, HEAD_DIM)], 2, i)
            return carry

        lax.fori_loop(0, ALONG, one, 0)

    spread_kv(0)
    spread_kv(1)
    halo_on_chip(0)

    def head(j, carry):
        got_blocks(kv.at[j], halo_recv.at[j], (core == 0) & (y == 1))
        for i in range(ALONG):
            got(qg.at[j, i], qg_sem.at[j, i])

        def half(part, carry):
            def one(n, carry):
                unit(j, 2 * part + lax.rem(x + n, 2))
                return carry

            lax.fori_loop(0, 2, one, 0)

            @pl.when(part == 0)
            def _():
                give_back(j)

                @pl.when(j + 2 < HEADS_KV)
                def _():
                    spread_kv(j + 2)

                @pl.when(j + 1 < HEADS_KV)
                def _():
                    halo_on_chip(j + 1)

            return carry

        lax.fori_loop(0, 2, half, 0)
        give_query(j)
        give_twin(j)

        @pl.when(j >= 1)
        def _():
            give_kv(j - 1)

        return carry

    lax.fori_loop(0, HEADS_KV, head, 0)
    give_kv(HEADS_KV - 1)

    for n in range(len(STEPS)):
        got(q_hbm.at[:, 0:3072], in_send.at[n])
    for j in range(HEADS_KV):
        got_blocks(back_in.at[j], cross_send.at[j], (core == 1) & (y == 1))
        got_blocks(back_in.at[j], halo_send.at[j], (core == 1) & (y == 0))
        got_blocks(back_in.at[j], back_send.at[j], (core == 0) & (y == 1))
        got_blocks(back_in.at[j], part_send.at[j], (core == 1) & (y == 0))
    for n, ref in enumerate((dq_hbm, dk_hbm, dv_hbm)):
        wide = ref.shape[1] // ALONG
        got(ref.at[:, 0:wide], own_sem.at[n])
        got(ref.at[:, 0 : 3 * wide], out_send.at[n])
        got(ref.at[:, 0 : 3 * wide], out_recv.at[n])


def write_out(*refs):
    sems = refs[-1]
    copies = []
    for n in range(3):
        rows = refs[n].shape[0] // 4
        for m in range(4):
            at = pl.ds(m * rows, rows)
            copies.append(pltpu.make_async_copy(refs[n].at[at], refs[3 + n].at[at], sems.at[n, m]))
    for copy in copies:
        copy.start()
    for copy in copies:
        copy.wait()


def local(queries, key_rows, value_rows, output_grad):
    anywhere = pl.BlockSpec(memory_space=pl.ANY)
    dma = pltpu.SemaphoreType.DMA
    blocks = BLOCKS + HALO
    wide = SPAN * ROWS
    held = pl.pallas_call(
        functools.partial(kernel, lax.axis_size("seq")),
        out_shape=[pltpu.VMEM(a.shape, a.dtype) for a in (queries, key_rows, value_rows)],
        in_specs=[anywhere] * 4,
        out_specs=[anywhere] * 3,
        scratch_shapes=[
            pltpu.VMEM((HEADS_KV, ALONG, ROWS, 2 * PAIR), jnp.bfloat16),
            pltpu.VMEM((HEADS_KV, blocks, ROWS, 2 * HEAD_DIM), jnp.bfloat16),
            pltpu.VMEM((HEADS_KV, blocks, ROWS, 2 * HEAD_DIM), jnp.float32),
            pltpu.VMEM((HEADS_KV, blocks, ROWS, 2 * HEAD_DIM), jnp.bfloat16),
            pltpu.VMEM((HEADS_KV, HALO, ROWS, 2 * HEAD_DIM), jnp.bfloat16),
            pltpu.VMEM((HEADS_KV, ALONG, ROWS, 2 * HEAD_DIM), jnp.bfloat16),
            pltpu.VMEM((HEADS_KV, ALONG, ROWS, PAIR), jnp.bfloat16),
            pltpu.VMEM((wide, ROWS), jnp.float32),
            pltpu.VMEM((wide, ROWS), jnp.float32),
            pltpu.VMEM((wide, ROWS), jnp.bfloat16),
            pltpu.VMEM((wide, ROWS), jnp.bfloat16),
            dma((HEADS_KV, ALONG)),
            dma((HEADS_KV, ALONG)),
            dma((len(STEPS),)),
            *[dma((HEADS_KV,)) for _ in range(7)],
            dma((HEADS_KV, ALONG)),
            dma((3,)),
            dma((3,)),
            dma((3,)),
        ],
        compiler_params=pltpu.CompilerParams(
            collective_id=0, has_side_effects=True, vmem_limit_bytes=52 * 2**20
        ),
        name="window_grads",
    )(queries, key_rows, value_rows, output_grad)
    held = [pltpu.with_memory_space_constraint(a, pltpu.VMEM) for a in held]
    return pl.pallas_call(
        write_out,
        out_shape=[jax.ShapeDtypeStruct(a.shape, a.dtype) for a in (queries, key_rows, value_rows)],
        in_specs=[anywhere] * 3,
        out_specs=[anywhere] * 3,
        scratch_shapes=[dma((3, 4))],
        compiler_params=pltpu.CompilerParams(vmem_limit_bytes=4 * 2**20),
        name="write_out",
    )(*held)


def solution(mesh):
    placed = P(("seq", "head"), None)
    return jax.shard_map(
        local, mesh=mesh, in_specs=(placed,) * 4, out_specs=(placed,) * 3, check_vma=False
    )
```

```python
import functools
import math

import jax
import jax.numpy as jnp
from jax import lax
from jax.experimental import pallas as pl
from jax.experimental.pallas import tpu as pltpu
from jax.sharding import PartitionSpec as P

HEAD_DIM = 128
WINDOW = 1024
GROUP = 2
SCALE = 168.0 ** (-0.5)
LOG2E = math.log2(math.e)
NEG = -1e30

ROWS = 256
HALO = WINDOW // ROWS
SPAN = HALO + 1
ALONG = 4
BLOCKS = 8
HEADS_KV = 4
PAIR = GROUP * HEAD_DIM
MESH = pl.DeviceIdType.MESH
STEPS = (2, 1, 3)


def fold(op, value):
    out = value[0:8]
    for begin in range(8, value.shape[0], 8):
        out = op(out, value[begin : begin + 8])
    return out


def kernel(
    seq_count,
    q_hbm,
    k_hbm,
    v_hbm,
    g_hbm,
    dq_hbm,
    dk_hbm,
    dv_hbm,
    qg,
    kv,
    dkv,
    dkv_low,
    back_in,
    part_in,
    dq_low,
    s_two,
    g_two,
    p_low,
    s_low,
    qg_sem,
    kv_sem,
    in_send,
    cross_send,
    cross_recv,
    halo_send,
    halo_recv,
    back_send,
    back_recv,
    part_send,
    part_recv,
    out_send,
    out_recv,
    own_sem,
):
    s, h = lax.axis_index("seq"), lax.axis_index("head")
    x, y = h // 2, lax.rem(h, 2)
    core = lax.rem(s, 2)
    mate = s + 1 - 2 * core
    other = lax.rem(s + 2 * core - 1 + seq_count, seq_count)
    others = [(other, x * 2 + half) for half in range(2)]
    peers = [lax.rem(x + dx, ALONG) * 2 + y for dx in STEPS]
    twin = (s, x * 2 + 1 - y)

    barrier = pltpu.get_barrier_semaphore()
    met = [(s, peer) for peer in peers] + [twin, (mate, h)] + others
    for device in met:
        pl.semaphore_signal(barrier, inc=1, device_id=device, device_id_type=MESH)
    pl.semaphore_wait(barrier, len(met))

    def push(src, dst, send, recv, device):
        pltpu.make_async_remote_copy(
            src_ref=src, dst_ref=dst, send_sem=send, recv_sem=recv, device_id=device, device_id_type=MESH
        ).start()

    def got(ref, sem):
        pltpu.make_async_copy(ref, ref, sem).wait()

    def got_blocks(ref, sem, fewer):
        @pl.when(fewer)
        def _():
            got(ref.at[1:4], sem)

        @pl.when(jnp.logical_not(fewer))
        def _():
            got(ref.at[0:4], sem)

    def cross_has(i, half):
        return (i < ALONG - 1) | (half == 0) | (core == 0)

    def kv_part(j, owner_x, part):
        col = pl.multiple_of((owner_x * HEADS_KV + j) * HEAD_DIM, HEAD_DIM)
        ref = (k_hbm, v_hbm)[part]
        return ref.at[:, pl.ds(col, HEAD_DIM)], kv.at[j, HALO + h, :, part * HEAD_DIM : (part + 1) * HEAD_DIM]

    def qg_part(j, owner_x, part, piece):
        col = pl.multiple_of((owner_x * HEADS_KV + j) * PAIR, PAIR)
        half = slice(piece * (ROWS // 2), (piece + 1) * (ROWS // 2))
        ref = (q_hbm, g_hbm)[part]
        return ref.at[half, pl.ds(col, PAIR)], qg.at[j, x, half, part * PAIR : (part + 1) * PAIR]

    def push_kv(j):
        for part in range(2):
            for n, peer in enumerate(peers):
                src, dst = kv_part(j, peer // 2, part)
                push(src, dst, in_send.at[n], kv_sem.at[j, x], (s, peer))

    def push_qg(j):
        for group in ((0,), (1, 2)):
            for piece in range(2):
                for part in range(2):
                    for n in group:
                        src, dst = qg_part(j, peers[n] // 2, part, piece)
                        push(src, dst, in_send.at[n], qg_sem.at[j, x], (s, peers[n]))

    push_kv(0)
    for j in range(HEADS_KV):

        @pl.when(cross_has(x, y))
        def _(j=j):
            for part in range(2):
                src, dst = kv_part(j, x, part)
                push(src, dst, cross_send.at[j], cross_recv.at[j], twin)

    push_kv(1)
    push_qg(0)
    push_kv(2)
    push_qg(1)
    push_kv(3)
    push_qg(2)
    push_qg(3)

    def take_own(j, carry):
        for part in range(2):
            src, dst = kv_part(j, x, part)
            pltpu.make_async_copy(src, dst, kv_sem.at[j, x]).start()
            for piece in range(2):
                src, dst = qg_part(j, x, part, piece)
                pltpu.make_async_copy(src, dst, qg_sem.at[j, x]).start()
        return carry

    lax.fori_loop(0, HEADS_KV, take_own, 0)

    def clear(b, carry):
        for j in range(HEADS_KV):
            dkv[j, b] = jnp.zeros((ROWS, 2 * HEAD_DIM), jnp.float32)
        return carry

    lax.fori_loop(0, BLOCKS + HALO, clear, 0)

    def spread_kv(j):
        for i in range(ALONG):
            got(kv.at[j, HALO + 2 * i + y], kv_sem.at[j, i])
        for dx in STEPS:
            i = lax.rem(x + dx, ALONG)

            @pl.when(cross_has(i, y))
            def _(i=i):
                block = kv.at[j, HALO + 2 * i + y]
                push(block, block, cross_send.at[j], cross_recv.at[j], twin)

        def send_halo(i, half):
            src, dst = kv.at[j, BLOCKS + 2 * i + y], kv.at[j, 2 * i + y]
            push(src, dst, halo_send.at[j], halo_recv.at[j], others[half])

        @pl.when(core == 1)
        def _():
            for i in range(2):
                send_halo(i, 0)
            send_halo(1, 1)

            @pl.when(y == 1)
            def _():
                send_halo(0, 1)

    def halo_on_chip(j):
        got_blocks(kv.at[j], cross_recv.at[j], (core == 1) & (y == 0))

        @pl.when(core == 0)
        def _():
            for b in range(HALO):
                push(kv.at[j, BLOCKS + b], kv.at[j, b], halo_send.at[j], halo_recv.at[j], (mate, h))

    key_row = lax.broadcasted_iota(jnp.int32, (ROWS, ROWS), 0)
    query_col = lax.broadcasted_iota(jnp.int32, (ROWS, ROWS), 1)

    nt = (((1,), (1,)), ((), ()))
    nn = (((1,), (0,)), ((), ()))
    tn = (((0,), (0,)), ((), ()))

    def unit(j, i):
        r = 2 * i + y
        keys = kv[j, pl.ds(r, SPAN), :, 0:HEAD_DIM].reshape(SPAN * ROWS, HEAD_DIM)
        values = kv[j, pl.ds(r, SPAN), :, HEAD_DIM:].reshape(SPAN * ROWS, HEAD_DIM)
        inside = [(s > 0) | (r + c >= HALO) for c in range(HALO)]
        for hh in range(GROUP):
            query = qg[j, i, :, hh * HEAD_DIM : (hh + 1) * HEAD_DIM]
            grad = qg[j, i, :, PAIR + hh * HEAD_DIM : PAIR + (hh + 1) * HEAD_DIM]
            s_two[hh] = lax.dot_general(keys, query, nt, preferred_element_type=jnp.float32)
            g_two[hh] = lax.dot_general(values, grad, nt, preferred_element_type=jnp.float32)
        for hh in range(GROUP):
            cols = slice(hh * ROWS, (hh + 1) * ROWS)
            s_buf, g_buf = s_two.at[hh], g_two.at[hh]

            peak = jnp.full((8, ROWS), NEG, jnp.float32)
            for c in range(SPAN):
                part = s_buf[c * ROWS : (c + 1) * ROWS]
                if c in (0, HALO):
                    seen = key_row > query_col if c == 0 else key_row <= query_col
                    part = jnp.where(seen, part, NEG)
                    s_buf[c * ROWS : (c + 1) * ROWS] = part
                highest = fold(jnp.maximum, part)
                peak = jnp.maximum(peak, highest if c == HALO else jnp.where(inside[c], highest, NEG))
            peak = jnp.max(peak, axis=0, keepdims=True)
            peaks = [jnp.where(inside[c], peak, -NEG) for c in range(HALO)] + [peak]
            total = jnp.zeros((8, ROWS), jnp.float32)
            centre = jnp.zeros((8, ROWS), jnp.float32)
            step = 64
            for begin in range(0, SPAN * ROWS, step):
                at = slice(begin, begin + step)
                raised = jnp.exp2((s_buf[at] - peaks[begin // ROWS]) * (SCALE * LOG2E))
                s_buf[at] = raised
                total = total + fold(jnp.add, raised)
                centre = centre + fold(jnp.add, raised * g_buf[at])
            scale = 1.0 / jnp.sum(total, axis=0, keepdims=True)
            centre = jnp.sum(centre, axis=0, keepdims=True) * scale
            for begin in range(0, SPAN * ROWS, step):
                at = slice(begin, begin + step)
                prob = s_buf[at] * scale
                p_low[at, cols] = prob.astype(jnp.bfloat16)
                s_low[at, cols] = (prob * (g_buf[at] - centre)).astype(jnp.bfloat16)
            query_part = lax.dot_general(s_low[:, cols], keys, tn, preferred_element_type=jnp.float32)
            dq_low[j, i, :, hh * HEAD_DIM : (hh + 1) * HEAD_DIM] = (query_part * SCALE).astype(jnp.bfloat16)
        for low, first, out in ((s_low, 0, 0), (p_low, PAIR, HEAD_DIM)):
            heads = [qg[j, i, :, first + hh * HEAD_DIM : first + (hh + 1) * HEAD_DIM] for hh in range(GROUP)]
            both = jnp.concatenate(heads, axis=0)
            whole = lax.dot_general(low[...], both, nn, preferred_element_type=jnp.float32)
            for c in range(SPAN):
                dkv[j, r + c, :, out : out + HEAD_DIM] += whole[c * ROWS : (c + 1) * ROWS]

    def rounded(j, b, extras=()):
        key_grad = dkv[j, b, :, 0:HEAD_DIM] * SCALE
        value_grad = dkv[j, b, :, HEAD_DIM:]
        for extra in extras:
            key_grad = key_grad + extra[:, 0:HEAD_DIM].astype(jnp.float32)
            value_grad = value_grad + extra[:, HEAD_DIM:].astype(jnp.float32)
        dkv_low[j, b, :, 0:HEAD_DIM] = key_grad.astype(jnp.bfloat16)
        dkv_low[j, b, :, HEAD_DIM:] = value_grad.astype(jnp.bfloat16)

    def give_back(j):
        def one(b, carry):
            rounded(j, b)
            block = dkv_low.at[j, b]

            @pl.when(core == 1)
            def _():
                push(block, back_in.at[j, b], back_send.at[j], back_recv.at[j], (mate, h))

            @pl.when((core == 0) & (b >= y))
            def _():
                slot = 2 * y + b // 2
                to = (other, x * 2 + lax.rem(b, 2))
                push(block, back_in.at[j, slot], back_send.at[j], back_recv.at[j], to)

            return carry

        lax.fori_loop(0, HALO, one, 0)

    def give_twin(j):
        @pl.when(core == 0)
        def _():
            got(back_in.at[j], back_recv.at[j])

        def one(n, carry):
            i = lax.rem(x + jnp.where(n == 0, 2, jnp.where(n == 1, 1, jnp.where(n == 2, 3, 0))), ALONG)
            b = HALO + 2 * i + 1 - y

            @pl.when((core == 0) & (i >= 2))
            def _():
                rounded(j, b, (back_in[j, lax.rem(2 * i + 1 - y, HALO)],))

            @pl.when((core == 1) | (i < 2))
            def _():
                rounded(j, b)

            @pl.when(cross_has(i, 1 - y))
            def _():
                push(dkv_low.at[j, b], part_in.at[j, i], part_send.at[j], part_recv.at[j, i], twin)

            return carry

        lax.fori_loop(0, ALONG, one, 0)

    def give(src, dst, n, owner_x):
        @pl.when(owner_x == x)
        def _():
            pltpu.make_async_copy(src, dst, own_sem.at[n]).start()

        @pl.when(owner_x != x)
        def _():
            push(src, dst, out_send.at[n], out_recv.at[n], (s, owner_x * 2 + y))

    def give_query(j):
        col = pl.multiple_of((x * HEADS_KV + j) * PAIR, PAIR)
        for piece in range(2):
            half = slice(piece * (ROWS // 2), (piece + 1) * (ROWS // 2))
            for dx in STEPS + (0,):
                i = lax.rem(x + dx, ALONG)
                give(dq_low.at[j, i, half], dq_hbm.at[half, pl.ds(col, PAIR)], 0, i)

    def give_kv(j):
        @pl.when(core == 1)
        def _():
            got_blocks(back_in.at[j], back_recv.at[j], y == 0)

        col = pl.multiple_of((x * HEADS_KV + j) * HEAD_DIM, HEAD_DIM)

        def one(n, carry):
            i = lax.rem(x + jnp.where(n == 0, 2, jnp.where(n == 1, 1, jnp.where(n == 2, 3, 0))), ALONG)
            b = HALO + 2 * i + y
            slot = lax.rem(i, 2)

            @pl.when(cross_has(i, y))
            def _():
                got(part_in.at[j, i], part_recv.at[j, i])

            @pl.when(i < 2)
            def _():
                rounded(j, b, (part_in[j, i],))

            @pl.when((i >= 2) & (core == 0))
            def _():
                rounded(j, b, (part_in[j, i], back_in[j, lax.rem(2 * i + y, HALO)]))

            @pl.when((i == 2) & (core == 1) & (y == 0))
            def _():
                rounded(j, b, (part_in[j, i], back_in[j, slot]))

            @pl.when((i == 2) & (core == 1) & (y == 1))
            def _():
                rounded(j, b, (part_in[j, i], back_in[j, slot], back_in[j, 2 + slot]))

            @pl.when((i == 3) & (core == 1) & (y == 0))
            def _():
                rounded(j, b, (part_in[j, i], back_in[j, slot], back_in[j, 2 + slot]))

            @pl.when((i == 3) & (core == 1) & (y == 1))
            def _():
                rounded(j, b, (back_in[j, slot], back_in[j, 2 + slot]))

            give(dkv_low.at[j, b, :, 0:HEAD_DIM], dk_hbm.at[:, pl.ds(col, HEAD_DIM)], 1, i)
            give(dkv_low.at[j, b, :, HEAD_DIM:], dv_hbm.at[:, pl.ds(col, HEAD_DIM)], 2, i)
            return carry

        lax.fori_loop(0, ALONG, one, 0)

    spread_kv(0)
    spread_kv(1)
    halo_on_chip(0)

    def head(j, carry):
        got_blocks(kv.at[j], halo_recv.at[j], (core == 0) & (y == 1))
        def half(part, carry):
            def one(n, carry):
                i = 2 * part + lax.rem(x + n, 2)
                got(qg.at[j, i], qg_sem.at[j, i])
                unit(j, i)
                return carry

            lax.fori_loop(0, 2, one, 0)

            @pl.when(part == 0)
            def _():
                give_back(j)

                @pl.when(j + 2 < HEADS_KV)
                def _():
                    spread_kv(j + 2)

                @pl.when(j + 1 < HEADS_KV)
                def _():
                    halo_on_chip(j + 1)

            return carry

        lax.fori_loop(0, 2, half, 0)
        give_twin(j)
        give_query(j)

        @pl.when(j >= 1)
        def _():
            give_kv(j - 1)

        return carry

    lax.fori_loop(0, HEADS_KV, head, 0)
    give_kv(HEADS_KV - 1)

    for n in range(len(STEPS)):
        got(q_hbm.at[:, 0:3072], in_send.at[n])
    for j in range(HEADS_KV):
        got_blocks(back_in.at[j], cross_send.at[j], (core == 1) & (y == 1))
        got_blocks(back_in.at[j], halo_send.at[j], (core == 1) & (y == 0))
        got_blocks(back_in.at[j], back_send.at[j], (core == 0) & (y == 1))
        got_blocks(back_in.at[j], part_send.at[j], (core == 1) & (y == 0))
    for n, ref in enumerate((dq_hbm, dk_hbm, dv_hbm)):
        wide = ref.shape[1] // ALONG
        got(ref.at[:, 0:wide], own_sem.at[n])
        got(ref.at[:, 0 : 3 * wide], out_send.at[n])
        got(ref.at[:, 0 : 3 * wide], out_recv.at[n])


def write_out(*refs):
    sems = refs[-1]
    copies = []
    for n in range(3):
        rows = refs[n].shape[0] // 4
        for m in range(4):
            at = pl.ds(m * rows, rows)
            copies.append(pltpu.make_async_copy(refs[n].at[at], refs[3 + n].at[at], sems.at[n, m]))
    for copy in copies:
        copy.start()
    for copy in copies:
        copy.wait()


def local(queries, key_rows, value_rows, output_grad):
    anywhere = pl.BlockSpec(memory_space=pl.ANY)
    dma = pltpu.SemaphoreType.DMA
    blocks = BLOCKS + HALO
    wide = SPAN * ROWS
    held = pl.pallas_call(
        functools.partial(kernel, lax.axis_size("seq")),
        out_shape=[pltpu.VMEM(a.shape, a.dtype) for a in (queries, key_rows, value_rows)],
        in_specs=[anywhere] * 4,
        out_specs=[anywhere] * 3,
        scratch_shapes=[
            pltpu.VMEM((HEADS_KV, ALONG, ROWS, 2 * PAIR), jnp.bfloat16),
            pltpu.VMEM((HEADS_KV, blocks, ROWS, 2 * HEAD_DIM), jnp.bfloat16),
            pltpu.VMEM((HEADS_KV, blocks, ROWS, 2 * HEAD_DIM), jnp.float32),
            pltpu.VMEM((HEADS_KV, blocks, ROWS, 2 * HEAD_DIM), jnp.bfloat16),
            pltpu.VMEM((HEADS_KV, HALO, ROWS, 2 * HEAD_DIM), jnp.bfloat16),
            pltpu.VMEM((HEADS_KV, ALONG, ROWS, 2 * HEAD_DIM), jnp.bfloat16),
            pltpu.VMEM((HEADS_KV, ALONG, ROWS, PAIR), jnp.bfloat16),
            pltpu.VMEM((GROUP, wide, ROWS), jnp.float32),
            pltpu.VMEM((GROUP, wide, ROWS), jnp.float32),
            pltpu.VMEM((wide, GROUP * ROWS), jnp.bfloat16),
            pltpu.VMEM((wide, GROUP * ROWS), jnp.bfloat16),
            dma((HEADS_KV, ALONG)),
            dma((HEADS_KV, ALONG)),
            dma((len(STEPS),)),
            *[dma((HEADS_KV,)) for _ in range(7)],
            dma((HEADS_KV, ALONG)),
            dma((3,)),
            dma((3,)),
            dma((3,)),
        ],
        compiler_params=pltpu.CompilerParams(
            collective_id=0, has_side_effects=True, vmem_limit_bytes=52 * 2**20
        ),
        name="window_grads",
    )(queries, key_rows, value_rows, output_grad)
    held = [pltpu.with_memory_space_constraint(a, pltpu.VMEM) for a in held]
    return pl.pallas_call(
        write_out,
        out_shape=[jax.ShapeDtypeStruct(a.shape, a.dtype) for a in (queries, key_rows, value_rows)],
        in_specs=[anywhere] * 3,
        out_specs=[anywhere] * 3,
        scratch_shapes=[dma((3, 4))],
        compiler_params=pltpu.CompilerParams(vmem_limit_bytes=4 * 2**20),
        name="write_out",
    )(*held)


def solution(mesh):
    placed = P(("seq", "head"), None)
    return jax.shard_map(
        local, mesh=mesh, in_specs=(placed,) * 4, out_specs=(placed,) * 3, check_vma=False
    )
```

```python
import functools
import math

import jax
import jax.numpy as jnp
from jax import lax
from jax.experimental import pallas as pl
from jax.experimental.pallas import tpu as pltpu
from jax.sharding import PartitionSpec as P

HEAD_DIM = 128
WINDOW = 1024
GROUP = 2
SCALE = 168.0 ** (-0.5)
LOG2E = math.log2(math.e)
NEG = -1e30

ROWS = 256
HALO = WINDOW // ROWS
SPAN = HALO + 1
ALONG = 4
BLOCKS = 8
HEADS_KV = 4
PAIR = GROUP * HEAD_DIM
MESH = pl.DeviceIdType.MESH
STEPS = (2, 1, 3)


def fold(op, value):
    out = value[0:8]
    for begin in range(8, value.shape[0], 8):
        out = op(out, value[begin : begin + 8])
    return out


def kernel(
    seq_count,
    q_hbm,
    k_hbm,
    v_hbm,
    g_hbm,
    dq_hbm,
    dk_hbm,
    dv_hbm,
    qg,
    kv,
    dkv,
    dkv_low,
    back_in,
    part_in,
    dq_low,
    s_two,
    g_two,
    p_low,
    s_low,
    qg_sem,
    kv_sem,
    in_send,
    cross_send,
    cross_recv,
    halo_send,
    halo_recv,
    back_send,
    back_recv,
    part_send,
    part_recv,
    out_send,
    out_recv,
    own_sem,
):
    s, h = lax.axis_index("seq"), lax.axis_index("head")
    x, y = h // 2, lax.rem(h, 2)
    core = lax.rem(s, 2)
    mate = s + 1 - 2 * core
    other = lax.rem(s + 2 * core - 1 + seq_count, seq_count)
    others = [(other, x * 2 + half) for half in range(2)]
    peers = [lax.rem(x + dx, ALONG) * 2 + y for dx in STEPS]
    twin = (s, x * 2 + 1 - y)

    barrier = pltpu.get_barrier_semaphore()
    met = [(s, peer) for peer in peers] + [twin, (mate, h)] + others
    for device in met:
        pl.semaphore_signal(barrier, inc=1, device_id=device, device_id_type=MESH)
    pl.semaphore_wait(barrier, len(met))

    def push(src, dst, send, recv, device):
        pltpu.make_async_remote_copy(
            src_ref=src, dst_ref=dst, send_sem=send, recv_sem=recv, device_id=device, device_id_type=MESH
        ).start()

    def got(ref, sem):
        pltpu.make_async_copy(ref, ref, sem).wait()

    def got_blocks(ref, sem, fewer):
        @pl.when(fewer)
        def _():
            got(ref.at[1:4], sem)

        @pl.when(jnp.logical_not(fewer))
        def _():
            got(ref.at[0:4], sem)

    def cross_has(i, half):
        return (i < ALONG - 1) | (half == 0) | (core == 0)

    def kv_part(j, owner_x, part):
        col = pl.multiple_of((owner_x * HEADS_KV + j) * HEAD_DIM, HEAD_DIM)
        ref = (k_hbm, v_hbm)[part]
        return ref.at[:, pl.ds(col, HEAD_DIM)], kv.at[j, HALO + h, :, part * HEAD_DIM : (part + 1) * HEAD_DIM]

    def qg_part(j, owner_x, part, piece):
        col = pl.multiple_of((owner_x * HEADS_KV + j) * PAIR, PAIR)
        half = slice(piece * (ROWS // 2), (piece + 1) * (ROWS // 2))
        ref = (q_hbm, g_hbm)[part]
        return ref.at[half, pl.ds(col, PAIR)], qg.at[j, x, half, part * PAIR : (part + 1) * PAIR]

    def push_kv(j):
        for part in range(2):
            for n, peer in enumerate(peers):
                src, dst = kv_part(j, peer // 2, part)
                push(src, dst, in_send.at[n], kv_sem.at[j, x], (s, peer))

    def push_qg(j):
        for group in ((0,), (1, 2)):
            for piece in range(2):
                for part in range(2):
                    for n in group:
                        src, dst = qg_part(j, peers[n] // 2, part, piece)
                        push(src, dst, in_send.at[n], qg_sem.at[j, x], (s, peers[n]))

    push_kv(0)
    for j in range(HEADS_KV):

        @pl.when(cross_has(x, y))
        def _(j=j):
            for part in range(2):
                src, dst = kv_part(j, x, part)
                push(src, dst, cross_send.at[j], cross_recv.at[j], twin)

    push_kv(1)
    push_qg(0)
    push_kv(2)
    push_qg(1)
    push_kv(3)
    push_qg(2)
    push_qg(3)

    def take_own(j, carry):
        for part in range(2):
            src, dst = kv_part(j, x, part)
            pltpu.make_async_copy(src, dst, kv_sem.at[j, x]).start()
            for piece in range(2):
                src, dst = qg_part(j, x, part, piece)
                pltpu.make_async_copy(src, dst, qg_sem.at[j, x]).start()
        return carry

    lax.fori_loop(0, HEADS_KV, take_own, 0)

    def clear(b, carry):
        for j in range(HEADS_KV):
            dkv[j, b] = jnp.zeros((ROWS, 2 * HEAD_DIM), jnp.float32)
        return carry

    lax.fori_loop(0, BLOCKS + HALO, clear, 0)

    def spread_kv(j):
        for i in range(ALONG):
            got(kv.at[j, HALO + 2 * i + y], kv_sem.at[j, i])
        for dx in STEPS:
            i = lax.rem(x + dx, ALONG)

            @pl.when(cross_has(i, y))
            def _(i=i):
                block = kv.at[j, HALO + 2 * i + y]
                push(block, block, cross_send.at[j], cross_recv.at[j], twin)

        def send_halo(i, half):
            src, dst = kv.at[j, BLOCKS + 2 * i + y], kv.at[j, 2 * i + y]
            push(src, dst, halo_send.at[j], halo_recv.at[j], others[half])

        @pl.when(core == 1)
        def _():
            for i in range(2):
                send_halo(i, 0)
            send_halo(1, 1)

            @pl.when(y == 1)
            def _():
                send_halo(0, 1)

    def halo_on_chip(j):
        got_blocks(kv.at[j], cross_recv.at[j], (core == 1) & (y == 0))

        @pl.when(core == 0)
        def _():
            for b in range(HALO):
                push(kv.at[j, BLOCKS + b], kv.at[j, b], halo_send.at[j], halo_recv.at[j], (mate, h))

    key_row = lax.broadcasted_iota(jnp.int32, (ROWS, ROWS), 0)
    query_col = lax.broadcasted_iota(jnp.int32, (ROWS, ROWS), 1)

    nt = (((1,), (1,)), ((), ()))
    nn = (((1,), (0,)), ((), ()))
    tn = (((0,), (0,)), ((), ()))

    def unit(j, i):
        r = 2 * i + y
        keys = kv[j, pl.ds(r, SPAN), :, 0:HEAD_DIM].reshape(SPAN * ROWS, HEAD_DIM)
        values = kv[j, pl.ds(r, SPAN), :, HEAD_DIM:].reshape(SPAN * ROWS, HEAD_DIM)
        inside = [(s > 0) | (r + c >= HALO) for c in range(HALO)]
        for hh in range(GROUP):
            query = qg[j, i, :, hh * HEAD_DIM : (hh + 1) * HEAD_DIM]
            grad = qg[j, i, :, PAIR + hh * HEAD_DIM : PAIR + (hh + 1) * HEAD_DIM]
            s_two[hh] = lax.dot_general(keys, query, nt, preferred_element_type=jnp.float32)
            g_two[hh] = lax.dot_general(values, grad, nt, preferred_element_type=jnp.float32)
        for hh in range(GROUP):
            cols = slice(hh * ROWS, (hh + 1) * ROWS)
            s_buf, g_buf = s_two.at[hh], g_two.at[hh]

            peak = jnp.full((8, ROWS), NEG, jnp.float32)
            for c in range(SPAN):
                part = s_buf[c * ROWS : (c + 1) * ROWS]
                if c in (0, HALO):
                    seen = key_row > query_col if c == 0 else key_row <= query_col
                    part = jnp.where(seen, part, NEG)
                    s_buf[c * ROWS : (c + 1) * ROWS] = part
                highest = fold(jnp.maximum, part)
                peak = jnp.maximum(peak, highest if c == HALO else jnp.where(inside[c], highest, NEG))
            peak = jnp.max(peak, axis=0, keepdims=True)
            peaks = [jnp.where(inside[c], peak, -NEG) for c in range(HALO)] + [peak]
            total = jnp.zeros((8, ROWS), jnp.float32)
            centre = jnp.zeros((8, ROWS), jnp.float32)
            step = 64
            for begin in range(0, SPAN * ROWS, step):
                at = slice(begin, begin + step)
                raised = jnp.exp2((s_buf[at] - peaks[begin // ROWS]) * (SCALE * LOG2E))
                s_buf[at] = raised
                total = total + fold(jnp.add, raised)
                centre = centre + fold(jnp.add, raised * g_buf[at])
            scale = 1.0 / jnp.sum(total, axis=0, keepdims=True)
            centre = jnp.sum(centre, axis=0, keepdims=True) * scale
            for begin in range(0, SPAN * ROWS, step):
                at = slice(begin, begin + step)
                prob = s_buf[at] * scale
                p_low[at, cols] = prob.astype(jnp.bfloat16)
                s_low[at, cols] = (prob * (g_buf[at] - centre)).astype(jnp.bfloat16)
            query_part = lax.dot_general(s_low[:, cols], keys, tn, preferred_element_type=jnp.float32)
            dq_low[j, i, :, hh * HEAD_DIM : (hh + 1) * HEAD_DIM] = (query_part * SCALE).astype(jnp.bfloat16)
        for low, first, out in ((s_low, 0, 0), (p_low, PAIR, HEAD_DIM)):
            heads = [qg[j, i, :, first + hh * HEAD_DIM : first + (hh + 1) * HEAD_DIM] for hh in range(GROUP)]
            both = jnp.concatenate(heads, axis=0)
            whole = lax.dot_general(low[...], both, nn, preferred_element_type=jnp.float32)
            for c in range(SPAN):
                dkv[j, r + c, :, out : out + HEAD_DIM] += whole[c * ROWS : (c + 1) * ROWS]

    def rounded(j, b, extras=()):
        key_grad = dkv[j, b, :, 0:HEAD_DIM] * SCALE
        value_grad = dkv[j, b, :, HEAD_DIM:]
        for extra in extras:
            key_grad = key_grad + extra[:, 0:HEAD_DIM].astype(jnp.float32)
            value_grad = value_grad + extra[:, HEAD_DIM:].astype(jnp.float32)
        dkv_low[j, b, :, 0:HEAD_DIM] = key_grad.astype(jnp.bfloat16)
        dkv_low[j, b, :, HEAD_DIM:] = value_grad.astype(jnp.bfloat16)

    def give_back(j):
        def one(b, carry):
            rounded(j, b)
            block = dkv_low.at[j, b]

            @pl.when(core == 1)
            def _():
                push(block, back_in.at[j, b], back_send.at[j], back_recv.at[j], (mate, h))

            @pl.when((core == 0) & (b >= y))
            def _():
                slot = 2 * y + b // 2
                to = (other, x * 2 + lax.rem(b, 2))
                push(block, back_in.at[j, slot], back_send.at[j], back_recv.at[j], to)

            return carry

        lax.fori_loop(0, HALO, one, 0)

    def give_twin(j):
        @pl.when(core == 0)
        def _():
            got(back_in.at[j], back_recv.at[j])

        def one(n, carry):
            i = lax.rem(x + jnp.where(n == 0, 2, jnp.where(n == 1, 1, jnp.where(n == 2, 3, 0))), ALONG)
            b = HALO + 2 * i + 1 - y

            @pl.when((core == 0) & (i >= 2))
            def _():
                rounded(j, b, (back_in[j, lax.rem(2 * i + 1 - y, HALO)],))

            @pl.when((core == 1) | (i < 2))
            def _():
                rounded(j, b)

            @pl.when(cross_has(i, 1 - y))
            def _():
                push(dkv_low.at[j, b], part_in.at[j, i], part_send.at[j], part_recv.at[j, i], twin)

            return carry

        lax.fori_loop(0, ALONG, one, 0)

    def give(src, dst, n, owner_x):
        @pl.when(owner_x == x)
        def _():
            pltpu.make_async_copy(src, dst, own_sem.at[n]).start()

        @pl.when(owner_x != x)
        def _():
            push(src, dst, out_send.at[n], out_recv.at[n], (s, owner_x * 2 + y))

    def give_query(j):
        col = pl.multiple_of((x * HEADS_KV + j) * PAIR, PAIR)
        for piece in range(2):
            half = slice(piece * (ROWS // 2), (piece + 1) * (ROWS // 2))
            for dx in STEPS + (0,):
                i = lax.rem(x + dx, ALONG)
                give(dq_low.at[j, i, half], dq_hbm.at[half, pl.ds(col, PAIR)], 0, i)

    def give_kv(j):
        @pl.when(core == 1)
        def _():
            got_blocks(back_in.at[j], back_recv.at[j], y == 0)

        col = pl.multiple_of((x * HEADS_KV + j) * HEAD_DIM, HEAD_DIM)

        def one(n, carry):
            i = lax.rem(x + jnp.where(n == 0, 2, jnp.where(n == 1, 1, jnp.where(n == 2, 3, 0))), ALONG)
            b = HALO + 2 * i + y
            slot = lax.rem(i, 2)

            @pl.when(cross_has(i, y))
            def _():
                got(part_in.at[j, i], part_recv.at[j, i])

            @pl.when(i < 2)
            def _():
                rounded(j, b, (part_in[j, i],))

            @pl.when((i >= 2) & (core == 0))
            def _():
                rounded(j, b, (part_in[j, i], back_in[j, lax.rem(2 * i + y, HALO)]))

            @pl.when((i == 2) & (core == 1) & (y == 0))
            def _():
                rounded(j, b, (part_in[j, i], back_in[j, slot]))

            @pl.when((i == 2) & (core == 1) & (y == 1))
            def _():
                rounded(j, b, (part_in[j, i], back_in[j, slot], back_in[j, 2 + slot]))

            @pl.when((i == 3) & (core == 1) & (y == 0))
            def _():
                rounded(j, b, (part_in[j, i], back_in[j, slot], back_in[j, 2 + slot]))

            @pl.when((i == 3) & (core == 1) & (y == 1))
            def _():
                rounded(j, b, (back_in[j, slot], back_in[j, 2 + slot]))

            give(dkv_low.at[j, b, :, 0:HEAD_DIM], dk_hbm.at[:, pl.ds(col, HEAD_DIM)], 1, i)
            give(dkv_low.at[j, b, :, HEAD_DIM:], dv_hbm.at[:, pl.ds(col, HEAD_DIM)], 2, i)
            return carry

        lax.fori_loop(0, ALONG, one, 0)

    spread_kv(0)
    spread_kv(1)
    halo_on_chip(0)

    def head(j, carry):
        got_blocks(kv.at[j], halo_recv.at[j], (core == 0) & (y == 1))
        def half(part, carry):
            for n in range(2):
                i = 2 * part + lax.rem(x + n, 2)
                got(qg.at[j, i], qg_sem.at[j, i])
                unit(j, i)

            @pl.when(part == 0)
            def _():
                give_back(j)

                @pl.when(j + 2 < HEADS_KV)
                def _():
                    spread_kv(j + 2)

                @pl.when(j + 1 < HEADS_KV)
                def _():
                    halo_on_chip(j + 1)

            return carry

        lax.fori_loop(0, 2, half, 0)
        give_twin(j)
        give_query(j)

        @pl.when(j >= 1)
        def _():
            give_kv(j - 1)

        return carry

    lax.fori_loop(0, HEADS_KV, head, 0)
    give_kv(HEADS_KV - 1)

    for n in range(len(STEPS)):
        got(q_hbm.at[:, 0:3072], in_send.at[n])
    for j in range(HEADS_KV):
        got_blocks(back_in.at[j], cross_send.at[j], (core == 1) & (y == 1))
        got_blocks(back_in.at[j], halo_send.at[j], (core == 1) & (y == 0))
        got_blocks(back_in.at[j], back_send.at[j], (core == 0) & (y == 1))
        got_blocks(back_in.at[j], part_send.at[j], (core == 1) & (y == 0))
    for n, ref in enumerate((dq_hbm, dk_hbm, dv_hbm)):
        wide = ref.shape[1] // ALONG
        got(ref.at[:, 0:wide], own_sem.at[n])
        got(ref.at[:, 0 : 3 * wide], out_send.at[n])
        got(ref.at[:, 0 : 3 * wide], out_recv.at[n])


def write_out(*refs):
    sems = refs[-1]
    copies = []
    for n in range(3):
        rows = refs[n].shape[0] // 4
        for m in range(4):
            at = pl.ds(m * rows, rows)
            copies.append(pltpu.make_async_copy(refs[n].at[at], refs[3 + n].at[at], sems.at[n, m]))
    for copy in copies:
        copy.start()
    for copy in copies:
        copy.wait()


def local(queries, key_rows, value_rows, output_grad):
    anywhere = pl.BlockSpec(memory_space=pl.ANY)
    dma = pltpu.SemaphoreType.DMA
    blocks = BLOCKS + HALO
    wide = SPAN * ROWS
    held = pl.pallas_call(
        functools.partial(kernel, lax.axis_size("seq")),
        out_shape=[pltpu.VMEM(a.shape, a.dtype) for a in (queries, key_rows, value_rows)],
        in_specs=[anywhere] * 4,
        out_specs=[anywhere] * 3,
        scratch_shapes=[
            pltpu.VMEM((HEADS_KV, ALONG, ROWS, 2 * PAIR), jnp.bfloat16),
            pltpu.VMEM((HEADS_KV, blocks, ROWS, 2 * HEAD_DIM), jnp.bfloat16),
            pltpu.VMEM((HEADS_KV, blocks, ROWS, 2 * HEAD_DIM), jnp.float32),
            pltpu.VMEM((HEADS_KV, blocks, ROWS, 2 * HEAD_DIM), jnp.bfloat16),
            pltpu.VMEM((HEADS_KV, HALO, ROWS, 2 * HEAD_DIM), jnp.bfloat16),
            pltpu.VMEM((HEADS_KV, ALONG, ROWS, 2 * HEAD_DIM), jnp.bfloat16),
            pltpu.VMEM((HEADS_KV, ALONG, ROWS, PAIR), jnp.bfloat16),
            pltpu.VMEM((GROUP, wide, ROWS), jnp.float32),
            pltpu.VMEM((GROUP, wide, ROWS), jnp.float32),
            pltpu.VMEM((wide, GROUP * ROWS), jnp.bfloat16),
            pltpu.VMEM((wide, GROUP * ROWS), jnp.bfloat16),
            dma((HEADS_KV, ALONG)),
            dma((HEADS_KV, ALONG)),
            dma((len(STEPS),)),
            *[dma((HEADS_KV,)) for _ in range(7)],
            dma((HEADS_KV, ALONG)),
            dma((3,)),
            dma((3,)),
            dma((3,)),
        ],
        compiler_params=pltpu.CompilerParams(
            collective_id=0, has_side_effects=True, vmem_limit_bytes=52 * 2**20
        ),
        name="window_grads",
    )(queries, key_rows, value_rows, output_grad)
    held = [pltpu.with_memory_space_constraint(a, pltpu.VMEM) for a in held]
    return pl.pallas_call(
        write_out,
        out_shape=[jax.ShapeDtypeStruct(a.shape, a.dtype) for a in (queries, key_rows, value_rows)],
        in_specs=[anywhere] * 3,
        out_specs=[anywhere] * 3,
        scratch_shapes=[dma((3, 4))],
        compiler_params=pltpu.CompilerParams(vmem_limit_bytes=4 * 2**20),
        name="write_out",
    )(*held)


def solution(mesh):
    placed = P(("seq", "head"), None)
    return jax.shard_map(
        local, mesh=mesh, in_specs=(placed,) * 4, out_specs=(placed,) * 3, check_vma=False
    )
```
